32 devices in a mesh: slab: 2 (over y), ang: 4 (over z), row: 2 (over x), ch: 2 (over core).
Axes of the slice: x: 2, y: 2, z: 4, core: 2. Of those that a mesh axis runs over, the one named last changes fastest.
Arguments:
- projections: float32 [8, 64, 2048], P(('slab', 'ang'), 'row'), parts along dimension 0, may hold values from -6 to 6
- conv1_weight: float32 [8, 3, 3], P('ch'), may hold values from -2 to 2
- conv1_bias: float32 [8], P('ch'), may hold values from -0.5 to 0.5
- filter_taps: float32 [8, 2048], P('ch'), may hold values from -0.125 to 0.125
- conv2_weight: float32 [8, 3, 3], replicated, may hold values from -0.75 to 0.75
- cotangent: float32 [4, 4, 32, 2048], P(('slab', 'row'), None, ('ang', 'ch')), parts along dimension 0, may hold values from -0.0029296875 to 0.0029296875
Outputs:
- sinogram: float32 [4, 4, 32, 2048], P(('slab', 'row'), None, ('ang', 'ch')), parts along dimension 0
- grad_conv1: float32 [16, 3, 3], P(('slab', 'ch')), parts along dimension 0
- grad_bias: float32 [16], P(('slab', 'ch')), parts along dimension 0
- grad_taps: float32 [16, 2048], P(('slab', 'ch')), parts along dimension 0
- grad_conv2: float32 [16, 3, 3], P(('slab', 'ch')), parts along dimension 0
The draws below stay inside these ranges and needn't reach their ends.
There are 2 independent parts, one for each index of `slab`. The reference program is written for one: setup_inputs(seed, part) draws one part's arguments, and reference() takes and returns one part's arrays. A program takes and returns all parts, laid end to end along the dimension named above; an argument that names none is the same for every part. Nothing has to cross between parts.
All inputs are finite; a program needn't handle non-finite values.
Results may differ from the reference program's by a relative error of at most 0.00028.
Values sent between devices are 32-bit elements; how exact they have to be, the bound alone decides.
A program may use at most 64 MiB of HBM per device.

```python
import jax
import jax.numpy as jnp
from jax import lax

W = 2048
C = 8
RD = 32
A = 4
R = 64
N_ROW = 2


def steps_of(rng, extent, pieces, least, high):
    gain = 1.0
    for dim, shards_of in pieces:
        heights = jax.random.uniform(jax.random.fold_in(jax.random.fold_in(rng, 6), dim), (shards_of,), jnp.float32, least / len(pieces), high / len(pieces))
        gain = gain * jnp.repeat(jnp.exp(heights), extent[dim] // shards_of).reshape((-1,) + (1,) * (len(extent) - 1 - dim))
    return gain


def bell_draw(rng, dims, spread, most, split=(), kind=jnp.bfloat16):
    level = steps_of(rng, dims, split, -0.22, 0.18) if split else 1.0
    drawn = jax.random.normal(rng, dims, jnp.float32) * spread * level
    return jnp.minimum(jnp.maximum(drawn, -most), most).astype(kind)


def setup_inputs(seed: int = 0, part: int = 0) -> dict:
    splits = jax.random.split(jax.random.key(seed), 7)
    part_splits = jax.random.split(jax.random.fold_in(splits[6], part), 7)
    return {
        "projections": bell_draw(part_splits[0], (A, R, W), 1.0, 6.0, ((0, 4), (1, 2)), jnp.float32),
        "conv1_weight": bell_draw(splits[1], (C, 3, 3), 9 ** -0.5, 2.0, ((0, 2),), jnp.float32),
        "conv1_bias": jnp.clip(jax.random.uniform(splits[2], (C,), jnp.float32, -0.5, 0.5) * steps_of(splits[2], (C,), ((0, 2),), -0.4, 0.0), -0.5, 0.5),
        "filter_taps": bell_draw(splits[3], (C, W), W ** -0.5, 0.125, ((0, 2),), jnp.float32),
        "conv2_weight": bell_draw(splits[4], (C, 3, 3), (9 * C) ** -0.5, 0.75, (), jnp.float32),
        "cotangent": bell_draw(part_splits[5], (N_ROW, A, RD, W), 0.0005, 0.0029296875, ((0, 2), (2, 8)), jnp.float32),
    }


def row_shift(source, row_tap, col_tap):
    padded = jnp.pad(source, ((0, 0), (1, 1), (1, 1)))
    return padded[:, row_tap:row_tap + R, col_tap:col_tap + W]


def angle_shift(source, ang_tap, col_tap):
    rolled = jnp.roll(source, 1 - ang_tap, axis=0)
    padded = jnp.pad(rolled, ((0, 0), (0, 0), (1, 1)))
    return padded[:, :, col_tap:col_tap + W]


def reference(projections, conv1_weight, conv1_bias, filter_taps, conv2_weight, cotangent):
    upstream = jnp.transpose(cotangent, (1, 0, 2, 3)).reshape(A, R, W)

    def one_channel(running_sum, weights):
        first_kernel, bias_value, filter_row, second_kernel = weights
        pre_act = jnp.zeros((A, R, W), jnp.float32) + bias_value
        for row_tap in range(3):
            for col_tap in range(3):
                pre_act = pre_act + first_kernel[row_tap, col_tap] * row_shift(projections, row_tap, col_tap)
        gate_value = jax.nn.sigmoid(pre_act)
        hidden = pre_act * gate_value
        spec_hidden = jnp.fft.fft(hidden, axis=-1)
        spec_filter = jnp.fft.fft(filter_row)
        filtered = jnp.real(jnp.fft.ifft(jnp.conj(spec_filter) * spec_hidden, axis=-1)).astype(jnp.float32)
        out_part = jnp.zeros((A, R, W), jnp.float32)
        grad_filtered = jnp.zeros((A, R, W), jnp.float32)
        second_grads = []
        for ang_tap in range(3):
            for col_tap in range(3):
                shifted = angle_shift(filtered, ang_tap, col_tap)
                out_part = out_part + second_kernel[ang_tap, col_tap] * shifted
                second_grads.append(jnp.sum(upstream * shifted))
                grad_filtered = grad_filtered + second_kernel[ang_tap, col_tap] * angle_shift(upstream, 2 - ang_tap, 2 - col_tap)
        spec_back = jnp.fft.fft(grad_filtered, axis=-1)
        grad_hidden = jnp.real(jnp.fft.ifft(spec_filter * spec_back, axis=-1)).astype(jnp.float32)
        cross_spec = jnp.sum(jnp.conj(spec_back) * spec_hidden, axis=(0, 1))
        grad_taps = jnp.real(jnp.fft.ifft(cross_spec)).astype(jnp.float32)
        grad_pre = grad_hidden * gate_value * (1.0 + pre_act * (1.0 - gate_value))
        first_grads = []
        for row_tap in range(3):
            for col_tap in range(3):
                first_grads.append(jnp.sum(grad_pre * row_shift(projections, row_tap, col_tap)))
        grad_bias = jnp.sum(grad_pre)
        return running_sum + out_part, (jnp.stack(first_grads).reshape(3, 3), grad_bias, grad_taps, jnp.stack(second_grads).reshape(3, 3))

    summed, grads = lax.scan(one_channel, jnp.zeros((A, R, W), jnp.float32), (conv1_weight, conv1_bias, filter_taps, conv2_weight))
    sinogram = jnp.transpose(summed.reshape(A, N_ROW, RD, W), (1, 0, 2, 3))
    return (sinogram, grads[0], grads[1], grads[2], grads[3])
```

```python
import functools
import math

import jax
import jax.numpy as jnp
import numpy as np
import ml_dtypes
from jax import lax
from jax.experimental import pallas as pl
from jax.experimental.pallas import tpu as pltpu
from jax.sharding import PartitionSpec as P

MESH = pl.DeviceIdType.MESH
LANES = 128
SLOTS = 32


def twisted(value, k, n, sign):
    re, im = value
    if k == 0:
        return value
    if 4 * k == n:
        return (-im, re) if sign > 0 else (im, -re)
    if 8 * k == n:
        half = math.sqrt(0.5)
        return (half * (re - sign * im), half * (im + sign * re))
    if 8 * k == 3 * n:
        half = math.sqrt(0.5)
        return (half * (-re - sign * im), half * (-im + sign * re))
    cos = math.cos(2 * math.pi * k / n)
    sin = sign * math.sin(2 * math.pi * k / n)
    return (cos * re - sin * im, cos * im + sin * re)


def short_dft(values, sign):
    n = len(values)
    if n == 1:
        return values
    even = short_dft(values[0::2], sign)
    odd = short_dft(values[1::2], sign)
    low, high = [], []
    for k in range(n // 2):
        re, im = twisted(odd[k], k, n, sign)
        low.append((even[k][0] + re, even[k][1] + im))
        high.append((even[k][0] - re, even[k][1] - im))
    return low + high


def split_high_low(table):
    high = table.astype(ml_dtypes.bfloat16)
    low = (table - high.astype(np.float64)).astype(ml_dtypes.bfloat16)
    return high, low


def make_tables(length):
    outer = length // LANES
    index = np.arange(LANES)
    inner = 2 * np.pi * (np.outer(index, index) % LANES) / LANES
    cos, sin = np.cos(inner), np.sin(inner)
    forward = np.block([[cos, -sin], [sin, cos]])
    inverse = np.block([[cos, sin], [-sin, cos]]) / length
    twist = 2 * np.pi * np.outer(np.arange(outer), index) / length
    twist = np.repeat(twist, 8, axis=0)
    tables = np.stack([*split_high_low(forward), *split_high_low(inverse)])
    turns = np.stack([np.cos(twist), np.sin(twist)]).astype(np.float32)
    return tables, turns


def multiply(ref, start, rows, tables_ref, which):
    values = ref[pl.ds(start, rows), :]
    high = values.astype(jnp.bfloat16)
    low = (values - high.astype(jnp.float32)).astype(jnp.bfloat16)
    dot = functools.partial(jnp.dot, preferred_element_type=jnp.float32)
    table_high = tables_ref[which]
    ref[pl.ds(start, rows), :] = (
        dot(high, table_high) + dot(low, table_high) + dot(high, tables_ref[which + 1])
    )


def kernel(
    sizes,
    rows_ref, packed_ref, taps_ref, second_ref, cot_ref, tables_ref, turns_ref,
    sino_ref, taps_out_ref, small_out_ref,
    got, top, bottom, all_taps, all_packed, first_ref,
    cot_shift, proj_shift, spec_back, spec_hidden, spec_taps, work,
    back, slope, filt, partial, mixed,
    outgoing, incoming, collected,
    rows_send, rows_recv, edge_send, edge_recv, taps_send, taps_recv,
    packed_send, packed_recv, sum_send, sum_recv, gather_send, gather_recv, local_sem,
):
    ang_n, row_n, ch_n = sizes
    n = ang_n * row_n * ch_n
    angles, rq, columns = cot_ref.shape
    chans = second_ref.shape[0]
    chans_dev = taps_ref.shape[0]
    held = rows_ref.shape[0] - 2
    both = angles * rq
    half = both // 2
    outer = columns // LANES
    block = outer * half
    slab = lax.axis_index("slab")
    z, k, c0 = lax.axis_index("ang"), lax.axis_index("row"), lax.axis_index("ch")
    me = (z * row_n + k) * ch_n + c0

    def place(d):
        return (slab, d // (row_n * ch_n), d // ch_n % row_n, d % ch_n)

    barrier = pltpu.get_barrier_semaphore()

    @pl.loop(1, n)
    def _(o):
        pl.semaphore_signal(barrier, inc=1, device_id=place((me + o) % n), device_id_type=MESH)

    pl.semaphore_wait(barrier, n - 1)

    def rows_copy(o, slot, target):
        start = (target * ch_n + c0) * rq
        return pltpu.make_async_remote_copy(
            src_ref=rows_ref.at[pl.ds(start, rq + 2)], dst_ref=got.at[slot],
            send_sem=rows_send.at[o], recv_sem=rows_recv.at[slot],
            device_id=(slab, target, k, c0), device_id_type=MESH)

    def taps_copy(o, slot, target):
        return pltpu.make_async_remote_copy(
            src_ref=taps_ref, dst_ref=all_taps.at[slot],
            send_sem=taps_send.at[o], recv_sem=taps_recv.at[slot],
            device_id=(slab, z, k, target), device_id_type=MESH)

    def packed_copy(o, slot, target):
        return pltpu.make_async_remote_copy(
            src_ref=packed_ref, dst_ref=all_packed.at[slot],
            send_sem=packed_send.at[o], recv_sem=packed_recv.at[slot],
            device_id=(slab, z, k, target), device_id_type=MESH)

    def top_copy(slot):
        return pltpu.make_async_remote_copy(
            src_ref=rows_ref.at[held], dst_ref=top.at[slot],
            send_sem=edge_send.at[0], recv_sem=edge_recv.at[0, slot],
            device_id=(slab, 0, (k + 1) % row_n, 0), device_id_type=MESH)

    def bottom_copy(slot):
        return pltpu.make_async_remote_copy(
            src_ref=rows_ref.at[1], dst_ref=bottom.at[slot],
            send_sem=edge_send.at[1], recv_sem=edge_recv.at[1, slot],
            device_id=(slab, ang_n - 1, (k + row_n - 1) % row_n, ch_n - 1), device_id_type=MESH)

    for o in range(1, ch_n):
        taps_copy(o, c0, (c0 + o) % ch_n).start()
        packed_copy(o, c0, (c0 + o) % ch_n).start()
    sends_top = jnp.logical_and(c0 == 0, k < row_n - 1)
    sends_bottom = jnp.logical_and(c0 == ch_n - 1, k > 0)

    @pl.when(sends_top)
    def _():
        top_copy(z).start()

    @pl.when(sends_bottom)
    def _():
        bottom_copy(z).start()

    for o in range(1, ang_n):
        rows_copy(o, z, (z + o) % ang_n).start()

    got[z] = rows_ref[pl.ds((z * ch_n + c0) * rq, rq + 2)]
    all_taps[c0] = taps_ref[...]
    all_packed[c0] = packed_ref[...]

    column = lax.broadcasted_iota(jnp.int32, (both, columns), 1)
    first_col, last_col = column == 0, column == columns - 1

    def from_left(x):
        return jnp.where(first_col, 0.0, pltpu.roll(x, 1, 1))

    def from_right(x):
        return jnp.where(last_col, 0.0, pltpu.roll(x, columns - 1, 1))

    def cols(m):
        return slice(m * LANES, (m + 1) * LANES)

    lo, hi = slice(0, half), slice(half, both)
    re_l, im_l = slice(0, LANES), slice(LANES, 2 * LANES)

    upstream = jnp.concatenate([cot_ref[a] for a in range(angles)], axis=0)
    for i in range(3):
        shift = (i - 1) * rq % both
        turned = pltpu.roll(upstream, shift, 0) if shift else upstream
        cot_shift[3 * i] = from_right(turned)
        cot_shift[3 * i + 1] = turned
        cot_shift[3 * i + 2] = from_left(turned)

    def store_forward(ref, start, values):
        for q, (re, im) in enumerate(short_dft(values, -1)):
            part = slice(q * half, (q + 1) * half)
            cos, sin = turns_ref[0, part, :], turns_ref[1, part, :]
            rows = pl.ds(start + q * half, half)
            ref[rows, re_l] = re * cos + im * sin
            ref[rows, im_l] = im * cos - re * sin

    def load_inverse(ref, start):
        values = []
        for q in range(outer):
            part = slice(q * half, (q + 1) * half)
            cos, sin = turns_ref[0, part, :], turns_ref[1, part, :]
            rows = pl.ds(start + q * half, half)
            re, im = ref[rows, re_l], ref[rows, im_l]
            values.append((re * cos - im * sin, im * cos + re * sin))
        return short_dft(values, 1)

    def start_of(c):
        return pl.multiple_of(c * block, block)

    @pl.loop(0, chans)
    def _(c):
        weights = [second_ref[c, t // 3, t % 3] for t in range(9)]
        values = []
        for m in range(outer):
            pair = []
            for rows in (lo, hi):
                total = weights[0] * cot_shift[0, rows, cols(m)]
                for t in range(1, 9):
                    total = total + weights[t] * cot_shift[t, rows, cols(m)]
                pair.append(total)
            values.append(tuple(pair))
        store_forward(spec_back, start_of(c), values)

    step = 4 * block
    for s in range(0, chans * block, step):
        multiply(spec_back, s, step, tables_ref, 0)

    for o in range(1, ch_n):
        source = (c0 + o) % ch_n
        taps_copy(o, source, source).wait_recv()
        packed_copy(o, source, source).wait_recv()
    load_weights = pltpu.make_async_copy(all_packed, first_ref, local_sem)
    load_weights.start()
    taps = jnp.concatenate([all_taps[h] for h in range(ch_n)], axis=0)
    zero = jnp.zeros((chans, LANES), jnp.float32)
    store_forward(spec_taps, 0, [(taps[:, cols(m)], zero) for m in range(outer)])
    multiply(spec_taps, 0, block, tables_ref, 0)

    def tap_row(q, c):
        row = spec_taps[pl.ds(q * half + c, 1), :]
        row = jnp.broadcast_to(row, (half, 2 * LANES))
        return row[:, re_l], row[:, im_l]

    @pl.loop(0, chans)
    def _(c):
        for q in range(outer):
            tr, ti = tap_row(q, c)
            rows = pl.ds(start_of(c) + q * half, half)
            gr, gi = spec_back[rows, re_l], spec_back[rows, im_l]
            work[rows, re_l] = tr * gr - ti * gi
            work[rows, im_l] = tr * gi + ti * gr

    for s in range(0, chans * block, step):
        multiply(work, s, step, tables_ref, 2)

    @pl.loop(0, chans)
    def _(c):
        for m, (re, im) in enumerate(load_inverse(work, start_of(c))):
            back[c, lo, cols(m)] = re
            back[c, hi, cols(m)] = im

    load_weights.wait()
    for o in range(1, ang_n):
        source = (z + o) % ang_n
        rows_copy(o, source, source).wait_recv()

    @pl.when(jnp.logical_and(jnp.logical_and(z == 0, c0 == 0), k > 0))
    def _():
        for a in range(ang_n):
            top_copy(a).wait_recv()
            got[a, 0] = top[a]

    @pl.when(jnp.logical_and(jnp.logical_and(z == ang_n - 1, c0 == ch_n - 1), k < row_n - 1))
    def _():
        for a in range(ang_n):
            bottom_copy(a).wait_recv()
            got[a, rq + 1] = bottom[a]

    for a in range(angles):
        for r in range(rq + 2):
            line = got[a, r]
            for i in range(3):
                q = r - i
                if 0 <= q < rq:
                    for m in range(outer):
                        proj_shift[3 * i + 1, a * rq + q : a * rq + q + 1, cols(m)] = line[m : m + 1, :]
    for i in range(3):
        centre = proj_shift[3 * i + 1]
        proj_shift[3 * i] = from_left(centre)
        proj_shift[3 * i + 2] = from_right(centre)

    @pl.loop(0, chans)
    def _(c):
        h, l = c // chans_dev, c % chans_dev
        weights = [first_ref[h, l, t] for t in range(10)]
        values = []
        for m in range(outer):
            pair = []
            for rows in (lo, hi):
                pre = weights[9] + weights[0] * proj_shift[0, rows, cols(m)]
                for t in range(1, 9):
                    pre = pre + weights[t] * proj_shift[t, rows, cols(m)]
                gate = 0.5 + 0.5 * jnp.tanh(0.5 * pre)
                slope[c, rows, cols(m)] = gate * (1.0 + pre * (1.0 - gate))
                pair.append(pre * gate)
            values.append(tuple(pair))
        store_forward(spec_hidden, start_of(c), values)

    for s in range(0, chans * block, step):
        multiply(spec_hidden, s, step, tables_ref, 0)
    work[pl.ds(chans * block, block), :] = jnp.zeros((block, 2 * LANES), jnp.float32)
    line_of = lax.broadcasted_iota(jnp.int32, (half, LANES), 0)

    def folded(value):
        return jnp.sum(value, axis=0, keepdims=True)


    @pl.loop(0, chans)
    def _(c):
        for q in range(outer):
            tr, ti = tap_row(q, c)
            rows = pl.ds(start_of(c) + q * half, half)
            gr, gi = spec_back[rows, re_l], spec_back[rows, im_l]
            hr, hi_ = spec_hidden[rows, re_l], spec_hidden[rows, im_l]
            work[rows, re_l] = tr * hr + ti * hi_
            work[rows, im_l] = tr * hi_ - ti * hr
            at = slice(chans * block + q * half, chans * block + (q + 1) * half)
            work[at, re_l] = jnp.where(line_of == c, folded(gr * hr + gi * hi_), work[at, re_l])
            work[at, im_l] = jnp.where(line_of == c, folded(gr * hi_ - gi * hr), work[at, im_l])

    for s in range(0, chans * block, step):
        multiply(work, s, step, tables_ref, 2)
    multiply(work, chans * block, block, tables_ref, 2)
    partial[...] = jnp.zeros(partial.shape, jnp.float32)

    @pl.loop(0, chans)
    def _(c):
        sums = [jnp.zeros((half, LANES), jnp.float32) for _ in range(9)]
        for m, (re, im) in enumerate(load_inverse(work, start_of(c))):
            filt[c, lo, cols(m)] = re
            filt[c, hi, cols(m)] = im
            for t in range(9):
                sums[t] = sums[t] + re * cot_shift[t, lo, cols(m)] + im * cot_shift[t, hi, cols(m)]
        for t in range(9):
            partial[c, 16 + t : 17 + t, :] = folded(sums[t])

    @pl.loop(0, chans)
    def _(c):
        sums = [jnp.zeros((half, LANES), jnp.float32) for _ in range(10)]
        for m in range(outer):
            for rows in (lo, hi):
                grad = back[c, rows, cols(m)] * slope[c, rows, cols(m)]
                for t in range(9):
                    sums[t] = sums[t] + grad * proj_shift[t, rows, cols(m)]
                sums[9] = sums[9] + grad
        for t in range(10):
            partial[c, t : t + 1, :] = folded(sums[t])

    small = lax.dot_general(
        jnp.ones((8, LANES), jnp.float32), partial[...].reshape(chans * SLOTS, LANES), (((1,), (1,)), ((), ())),
        precision=lax.Precision.HIGHEST, preferred_element_type=jnp.float32)
    width = chans_dev * SLOTS
    for m, (re, im) in enumerate(load_inverse(work, chans * block)):
        outgoing[m, 0:chans, :] = re
        h = m % ch_n
        outgoing[m, chans : chans + 1, :] = small[0:1, h * width : (h + 1) * width]

    def sum_copy(o, slot, target):
        return pltpu.make_async_remote_copy(
            src_ref=outgoing.at[target % outer], dst_ref=incoming.at[slot],
            send_sem=sum_send.at[o], recv_sem=sum_recv.at[slot],
            device_id=place(target), device_id_type=MESH)

    @pl.loop(1, n)
    def _(o):
        sum_copy(o, me, (me + o) % n).start()

    incoming[me] = outgoing[me % outer]

    @pl.loop(0, outer)
    def _(m):
        at = pl.ds(pl.multiple_of(m * LANES, LANES), LANES)
        for rows in (lo, hi):
            pieces = [filt[c, rows, at] for c in range(chans)]
            for t in range(9):
                total = second_ref[0, t // 3, t % 3] * pieces[0]
                for c in range(1, chans):
                    total = total + second_ref[c, t // 3, t % 3] * pieces[c]
                mixed[t, rows, at] = total

    sides = []
    for j in range(3):
        total = mixed[3 + j]
        for i in (0, 2):
            total = total + pltpu.roll(mixed[3 * i + j], -(i - 1) * rq % both, 0)
        sides.append(total)
    image = sides[1] + from_left(sides[0]) + from_right(sides[2])
    for a in range(angles):
        sino_ref[a] = image[a * rq : (a + 1) * rq]

    @pl.loop(1, n)
    def _(o):
        source = (me + o) % n
        sum_copy(o, source, source).wait_recv()

    total = incoming[0]
    for d in range(1, n):
        total = total + incoming[d]
    small_out_ref[...] = jnp.broadcast_to(total[chans : chans + 1], small_out_ref.shape)
    mine = me % outer
    group = me - mine
    collected[mine] = total[0:chans]

    def gather_copy(o, slot, target):
        return pltpu.make_async_remote_copy(
            src_ref=collected.at[mine], dst_ref=collected.at[slot],
            send_sem=gather_send.at[o], recv_sem=gather_recv.at[slot],
            device_id=place(group + target), device_id_type=MESH)

    @pl.loop(1, outer)
    def _(o):
        gather_copy(o, mine, (mine + o) % outer).start()

    @pl.loop(1, outer)
    def _(o):
        source = (mine + o) % outer
        gather_copy(o, source, source).wait_recv()

    for m in range(outer):
        taps_out_ref[:, cols(m)] = collected[m, pl.ds(c0 * chans_dev, chans_dev), :]

    for o in range(1, ang_n):
        rows_copy(o, z, (z + o) % ang_n).wait_send()
    for o in range(1, ch_n):
        taps_copy(o, c0, (c0 + o) % ch_n).wait_send()
        packed_copy(o, c0, (c0 + o) % ch_n).wait_send()

    @pl.when(sends_top)
    def _():
        top_copy(z).wait_send()

    @pl.when(sends_bottom)
    def _():
        bottom_copy(z).wait_send()

    @pl.loop(1, n)
    def _(o):
        sum_copy(o, me, (me + o) % n).wait_send()

    @pl.loop(1, outer)
    def _(o):
        gather_copy(o, mine, (mine + o) % outer).wait_send()


def on_device(sizes, tables, projections, conv1_weight, conv1_bias, filter_taps, conv2_weight, cotangent):
    ang_n, row_n, ch_n = sizes
    n = ang_n * row_n * ch_n
    _, held, columns = projections.shape
    chans_dev = conv1_weight.shape[0]
    chans = chans_dev * ch_n
    _, angles, rq, _ = cotangent.shape
    outer = columns // LANES
    both = angles * rq
    block = outer * both // 2
    rows = jnp.pad(projections[0], ((1, 1), (0, 0))).reshape(held + 2, outer, LANES)
    packed = jnp.concatenate([conv1_weight.reshape(chans_dev, 9), conv1_bias[:, None]], axis=1)
    packed = jnp.pad(packed, ((0, 0), (0, LANES - 10)))
    f32 = jnp.float32
    vmem = pl.BlockSpec(memory_space=pltpu.VMEM)
    dma = pltpu.SemaphoreType.DMA
    wide = (both, columns)
    image, taps_out, small = pl.pallas_call(
        functools.partial(kernel, sizes),
        out_shape=(
            jax.ShapeDtypeStruct((angles, rq, columns), f32),
            jax.ShapeDtypeStruct((chans_dev, columns), f32),
            jax.ShapeDtypeStruct((8, LANES), f32),
        ),
        in_specs=[vmem, vmem, vmem, pl.BlockSpec(memory_space=pltpu.SMEM), vmem, vmem, vmem],
        out_specs=(vmem, vmem, vmem),
        scratch_shapes=[
            pltpu.VMEM((ang_n, rq + 2, outer, LANES), f32),
            pltpu.VMEM((ang_n, outer, LANES), f32),
            pltpu.VMEM((ang_n, outer, LANES), f32),
            pltpu.VMEM((ch_n, chans_dev, columns), f32),
            pltpu.VMEM((ch_n, chans_dev, LANES), f32),
            pltpu.SMEM((ch_n, chans_dev, LANES), f32),
            pltpu.VMEM((9,) + wide, f32),
            pltpu.VMEM((9,) + wide, f32),
            pltpu.VMEM((chans * block, 2 * LANES), f32),
            pltpu.VMEM((chans * block, 2 * LANES), f32),
            pltpu.VMEM((block, 2 * LANES), f32),
            pltpu.VMEM(((chans + 1) * block, 2 * LANES), f32),
            pltpu.VMEM((chans,) + wide, f32),
            pltpu.VMEM((chans,) + wide, f32),
            pltpu.VMEM((chans,) + wide, f32),
            pltpu.VMEM((chans, SLOTS, LANES), f32),
            pltpu.VMEM((9,) + wide, f32),
            pltpu.VMEM((outer, chans + 1, LANES), f32),
            pltpu.VMEM((n, chans + 1, LANES), f32),
            pltpu.VMEM((outer, chans, LANES), f32),
            dma((ang_n,)), dma((ang_n,)), dma((2,)), dma((2, ang_n)),
            dma((ch_n,)), dma((ch_n,)), dma((ch_n,)), dma((ch_n,)),
            dma((n,)), dma((n,)), dma((outer,)), dma((outer,)), dma(()),
        ],
        compiler_params=pltpu.CompilerParams(
            collective_id=0, has_side_effects=True, vmem_limit_bytes=48 * 2**20
        ),
        name="tomography",
    )(rows, packed, filter_taps, conv2_weight, cotangent[0], *tables)
    grads = small[0].reshape(chans_dev, SLOTS)
    return (
        image[None],
        grads[:, 0:9].reshape(chans_dev, 3, 3),
        grads[:, 9],
        taps_out,
        grads[:, 16:25].reshape(chans_dev, 3, 3),
    )


def solution(mesh):
    sizes = tuple(mesh.shape[axis] for axis in ("ang", "row", "ch"))

    def whole(projections, conv1_weight, conv1_bias, filter_taps, conv2_weight, cotangent):
        tables = make_tables(projections.shape[-1])

        def local(*arrays):
            return on_device(sizes, tuple(jnp.asarray(t) for t in tables), *arrays)

        return jax.shard_map(
            local,
            mesh=mesh,
            in_specs=(
                P(("slab", "ang"), "row", None),
                P("ch", None, None),
                P("ch"),
                P("ch", None),
                P(),
                P(("slab", "row"), None, ("ang", "ch"), None),
            ),
            out_specs=(
                P(("slab", "row"), None, ("ang", "ch"), None),
                P(("slab", "ch"), None, None),
                P(("slab", "ch")),
                P(("slab", "ch"), None),
                P(("slab", "ch"), None, None),
            ),
            check_vma=False,
        )(projections, conv1_weight, conv1_bias, filter_taps, conv2_weight, cotangent)

    return whole
```

```python
import functools
import math

import jax
import jax.numpy as jnp
import numpy as np
import ml_dtypes
from jax import lax
from jax.experimental import pallas as pl
from jax.experimental.pallas import tpu as pltpu
from jax.sharding import PartitionSpec as P

MESH = pl.DeviceIdType.MESH
LANES = 128
SLOTS = 32


def twisted(value, k, n, sign):
    re, im = value
    if k == 0:
        return value
    if 4 * k == n:
        return (-im, re) if sign > 0 else (im, -re)
    if 8 * k == n:
        half = math.sqrt(0.5)
        return (half * (re - sign * im), half * (im + sign * re))
    if 8 * k == 3 * n:
        half = math.sqrt(0.5)
        return (half * (-re - sign * im), half * (-im + sign * re))
    cos = math.cos(2 * math.pi * k / n)
    sin = sign * math.sin(2 * math.pi * k / n)
    return (cos * re - sin * im, cos * im + sin * re)


def short_dft(values, sign):
    n = len(values)
    if n == 1:
        return values
    even = short_dft(values[0::2], sign)
    odd = short_dft(values[1::2], sign)
    low, high = [], []
    for k in range(n // 2):
        re, im = twisted(odd[k], k, n, sign)
        low.append((even[k][0] + re, even[k][1] + im))
        high.append((even[k][0] - re, even[k][1] - im))
    return low + high


def split_high_low(table):
    high = table.astype(ml_dtypes.bfloat16)
    low = (table - high.astype(np.float64)).astype(ml_dtypes.bfloat16)
    return high, low


def make_tables(length):
    outer = length // LANES
    index = np.arange(LANES)
    inner = 2 * np.pi * (np.outer(index, index) % LANES) / LANES
    cos, sin = np.cos(inner), np.sin(inner)
    forward = np.block([[cos, -sin], [sin, cos]])
    inverse = np.block([[cos, sin], [-sin, cos]]) / length
    twist = 2 * np.pi * np.outer(np.arange(outer), index) / length
    twist = np.repeat(twist, 8, axis=0)
    tables = np.stack([*split_high_low(forward), *split_high_low(inverse)])
    turns = np.stack([np.cos(twist), np.sin(twist)]).astype(np.float32)
    return tables, turns


def multiply(ref, start, rows, tables_ref, which):
    values = ref[pl.ds(start, rows), :]
    high = values.astype(jnp.bfloat16)
    low = (values - high.astype(jnp.float32)).astype(jnp.bfloat16)
    dot = functools.partial(jnp.dot, preferred_element_type=jnp.float32)
    table_high = tables_ref[which]
    ref[pl.ds(start, rows), :] = (
        dot(high, table_high) + dot(low, table_high) + dot(high, tables_ref[which + 1])
    )


def kernel(
    sizes,
    proj_hbm, first_hbm, bias_hbm, taps_hbm, second_ref, cot_hbm, tables_hbm, turns_hbm,
    sino_ref, first_out_ref, bias_out_ref, taps_out_ref, second_out_ref,
    proj_ref, first_vmem, bias_vmem, taps_ref, cot_ref, tables_ref, turns_ref,
    rows_ref, packed_ref, small_in, small_own,
    got, top, bottom, all_taps, all_packed, first_ref,
    cot_shift, proj_shift, spec_back, spec_hidden, spec_taps, work,
    back, slope, filt, partial, mixed,
    outgoing, incoming, collected,
    rows_send, rows_recv, edge_send, edge_recv, taps_send, taps_recv,
    packed_send, packed_recv, sum_send, sum_recv, gather_send, gather_recv, small_send, small_recv, load_sem, local_sem,
):
    ang_n, row_n, ch_n = sizes
    n = ang_n * row_n * ch_n
    angles, rq, columns = cot_ref.shape
    chans = second_ref.shape[2]
    chans_dev = taps_ref.shape[0]
    held = proj_ref.shape[0]
    both = angles * rq
    half = both // 2
    outer = columns // LANES
    block = outer * half
    slab = lax.axis_index("slab")
    z, k, c0 = lax.axis_index("ang"), lax.axis_index("row"), lax.axis_index("ch")
    me = (z * row_n + k) * ch_n + c0

    def place(d):
        return (slab, d // (row_n * ch_n), d // ch_n % row_n, d % ch_n)

    barrier = pltpu.get_barrier_semaphore()

    @pl.loop(1, n)
    def _(o):
        pl.semaphore_signal(barrier, inc=1, device_id=place((me + o) % n), device_id_type=MESH)

    loads = [
        pltpu.make_async_copy(source, target, load_sem.at[at])
        for at, (source, target) in enumerate((
            (proj_hbm, proj_ref), (first_hbm, first_vmem), (bias_hbm, bias_vmem),
            (taps_hbm, taps_ref), (cot_hbm, cot_ref), (tables_hbm, tables_ref),
            (turns_hbm, turns_ref)))
    ]
    for load in loads:
        load.start()

    def cols(m):
        return slice(m * LANES, (m + 1) * LANES)

    edge = jnp.zeros((outer, LANES), jnp.float32)
    rows_ref[0:outer, :] = edge
    rows_ref[(held + 1) * outer : (held + 2) * outer, :] = edge
    packed_ref[...] = jnp.zeros(packed_ref.shape, jnp.float32)
    loads[0].wait()
    for at in range(0, held, 8):
        for m in range(outer):
            rows_ref[pl.ds((at + 1) * outer + m, 8, stride=outer), :] = proj_ref[at : at + 8, cols(m)]
    loads[1].wait()
    loads[2].wait()
    for i in range(3):
        packed_ref[:, 3 * i : 3 * i + 3] = first_vmem[i]
    for l in range(chans_dev):
        packed_ref[l : l + 1, 9:10] = bias_vmem[0:1, l : l + 1]
    loads[3].wait()
    pl.semaphore_wait(barrier, n - 1)

    def rows_copy(o, slot, target):
        start = pl.multiple_of((target * ch_n + c0) * rq * outer, outer)
        return pltpu.make_async_remote_copy(
            src_ref=rows_ref.at[pl.ds(start, (rq + 2) * outer)], dst_ref=got.at[slot],
            send_sem=rows_send.at[o], recv_sem=rows_recv.at[slot],
            device_id=(slab, target, k, c0), device_id_type=MESH)

    def taps_copy(o, slot, target):
        return pltpu.make_async_remote_copy(
            src_ref=taps_ref, dst_ref=all_taps.at[slot],
            send_sem=taps_send.at[o], recv_sem=taps_recv.at[slot],
            device_id=(slab, z, k, target), device_id_type=MESH)

    def packed_copy(o, slot, target):
        return pltpu.make_async_remote_copy(
            src_ref=packed_ref, dst_ref=all_packed.at[slot],
            send_sem=packed_send.at[o], recv_sem=packed_recv.at[slot],
            device_id=(slab, z, k, target), device_id_type=MESH)

    def top_copy(slot):
        return pltpu.make_async_remote_copy(
            src_ref=rows_ref.at[pl.ds(held * outer, outer)], dst_ref=top.at[slot],
            send_sem=edge_send.at[0], recv_sem=edge_recv.at[0, slot],
            device_id=(slab, 0, (k + 1) % row_n, 0), device_id_type=MESH)

    def bottom_copy(slot):
        return pltpu.make_async_remote_copy(
            src_ref=rows_ref.at[pl.ds(outer, outer)], dst_ref=bottom.at[slot],
            send_sem=edge_send.at[1], recv_sem=edge_recv.at[1, slot],
            device_id=(slab, ang_n - 1, (k + row_n - 1) % row_n, ch_n - 1), device_id_type=MESH)

    for o in range(1, ch_n):
        taps_copy(o, c0, (c0 + o) % ch_n).start()
        packed_copy(o, c0, (c0 + o) % ch_n).start()
    sends_top = jnp.logical_and(c0 == 0, k < row_n - 1)
    sends_bottom = jnp.logical_and(c0 == ch_n - 1, k > 0)

    @pl.when(sends_top)
    def _():
        top_copy(z).start()

    @pl.when(sends_bottom)
    def _():
        bottom_copy(z).start()

    for o in range(1, ang_n):
        rows_copy(o, z, (z + o) % ang_n).start()

    mine_at = pl.multiple_of((z * ch_n + c0) * rq * outer, outer)
    got[z] = rows_ref[pl.ds(mine_at, (rq + 2) * outer), :]
    all_taps[c0] = taps_ref[...]
    all_packed[c0] = packed_ref[...]

    column = lax.broadcasted_iota(jnp.int32, (both, columns), 1)
    first_col, last_col = column == 0, column == columns - 1

    def from_left(x):
        return jnp.where(first_col, 0.0, pltpu.roll(x, 1, 1))

    def from_right(x):
        return jnp.where(last_col, 0.0, pltpu.roll(x, columns - 1, 1))

    lo, hi = slice(0, half), slice(half, both)
    re_l, im_l = slice(0, LANES), slice(LANES, 2 * LANES)

    loads[4].wait()
    upstream = jnp.concatenate([cot_ref[a] for a in range(angles)], axis=0)
    for i in range(3):
        shift = (i - 1) * rq % both
        turned = pltpu.roll(upstream, shift, 0) if shift else upstream
        cot_shift[3 * i] = from_right(turned)
        cot_shift[3 * i + 1] = turned
        cot_shift[3 * i + 2] = from_left(turned)

    def store_forward(ref, start, values):
        for q, (re, im) in enumerate(short_dft(values, -1)):
            part = slice(q * half, (q + 1) * half)
            cos, sin = turns_ref[0, part, :], turns_ref[1, part, :]
            rows = pl.ds(start + q * half, half)
            ref[rows, re_l] = re * cos + im * sin
            ref[rows, im_l] = im * cos - re * sin

    def load_inverse(ref, start):
        values = []
        for q in range(outer):
            part = slice(q * half, (q + 1) * half)
            cos, sin = turns_ref[0, part, :], turns_ref[1, part, :]
            rows = pl.ds(start + q * half, half)
            re, im = ref[rows, re_l], ref[rows, im_l]
            values.append((re * cos - im * sin, im * cos + re * sin))
        return short_dft(values, 1)

    def start_of(c):
        return pl.multiple_of(c * block, block)

    loads[5].wait()
    loads[6].wait()

    @pl.loop(0, chans)
    def _(c):
        weights = [second_ref[t // 3, t % 3, c] for t in range(9)]
        values = []
        for m in range(outer):
            pair = []
            for rows in (lo, hi):
                total = weights[0] * cot_shift[0, rows, cols(m)]
                for t in range(1, 9):
                    total = total + weights[t] * cot_shift[t, rows, cols(m)]
                pair.append(total)
            values.append(tuple(pair))
        store_forward(spec_back, start_of(c), values)

    step = 4 * block
    for s in range(0, chans * block, step):
        multiply(spec_back, s, step, tables_ref, 0)

    for o in range(1, ch_n):
        source = (c0 + o) % ch_n
        taps_copy(o, source, source).wait_recv()
        packed_copy(o, source, source).wait_recv()
    load_weights = pltpu.make_async_copy(all_packed, first_ref, local_sem)
    load_weights.start()
    taps = jnp.concatenate([all_taps[h] for h in range(ch_n)], axis=0)
    zero = jnp.zeros((chans, LANES), jnp.float32)
    store_forward(spec_taps, 0, [(taps[:, cols(m)], zero) for m in range(outer)])
    multiply(spec_taps, 0, block, tables_ref, 0)

    def tap_row(q, c):
        row = spec_taps[pl.ds(q * half + c, 1), :]
        row = jnp.broadcast_to(row, (half, 2 * LANES))
        return row[:, re_l], row[:, im_l]

    @pl.loop(0, chans)
    def _(c):
        for q in range(outer):
            tr, ti = tap_row(q, c)
            rows = pl.ds(start_of(c) + q * half, half)
            gr, gi = spec_back[rows, re_l], spec_back[rows, im_l]
            work[rows, re_l] = tr * gr - ti * gi
            work[rows, im_l] = tr * gi + ti * gr

    for s in range(0, chans * block, step):
        multiply(work, s, step, tables_ref, 2)

    @pl.loop(0, chans)
    def _(c):
        for m, (re, im) in enumerate(load_inverse(work, start_of(c))):
            back[c, lo, cols(m)] = re
            back[c, hi, cols(m)] = im

    load_weights.wait()
    for o in range(1, ang_n):
        source = (z + o) % ang_n
        rows_copy(o, source, source).wait_recv()

    @pl.when(jnp.logical_and(jnp.logical_and(z == 0, c0 == 0), k > 0))
    def _():
        for a in range(ang_n):
            top_copy(a).wait_recv()
            got[a, 0:outer, :] = top[a]

    @pl.when(jnp.logical_and(jnp.logical_and(z == ang_n - 1, c0 == ch_n - 1), k < row_n - 1))
    def _():
        for a in range(ang_n):
            bottom_copy(a).wait_recv()
            got[a, (rq + 1) * outer : (rq + 2) * outer, :] = bottom[a]

    for a in range(angles):
        for i in range(3):
            for m in range(outer):
                lines = got[a, pl.ds(i * outer + m, rq, stride=outer), :]
                proj_shift[3 * i + 1, a * rq : (a + 1) * rq, cols(m)] = lines
    for i in range(3):
        centre = proj_shift[3 * i + 1]
        proj_shift[3 * i] = from_left(centre)
        proj_shift[3 * i + 2] = from_right(centre)

    @pl.loop(0, chans)
    def _(c):
        h, l = c // chans_dev, c % chans_dev
        weights = [first_ref[h, l, t] for t in range(10)]
        values = []
        for m in range(outer):
            pair = []
            for rows in (lo, hi):
                pre = weights[9] + weights[0] * proj_shift[0, rows, cols(m)]
                for t in range(1, 9):
                    pre = pre + weights[t] * proj_shift[t, rows, cols(m)]
                gate = 0.5 + 0.5 * jnp.tanh(0.5 * pre)
                slope[c, rows, cols(m)] = gate * (1.0 + pre * (1.0 - gate))
                pair.append(pre * gate)
            values.append(tuple(pair))
        store_forward(spec_hidden, start_of(c), values)

    for s in range(0, chans * block, step):
        multiply(spec_hidden, s, step, tables_ref, 0)
    work[pl.ds(chans * block, block), :] = jnp.zeros((block, 2 * LANES), jnp.float32)
    line_of = lax.broadcasted_iota(jnp.int32, (half, LANES), 0)

    def folded(value):
        return jnp.sum(value, axis=0, keepdims=True)


    @pl.loop(0, chans)
    def _(c):
        for q in range(outer):
            tr, ti = tap_row(q, c)
            rows = pl.ds(start_of(c) + q * half, half)
            gr, gi = spec_back[rows, re_l], spec_back[rows, im_l]
            hr, hi_ = spec_hidden[rows, re_l], spec_hidden[rows, im_l]
            work[rows, re_l] = tr * hr + ti * hi_
            work[rows, im_l] = tr * hi_ - ti * hr
            at = slice(chans * block + q * half, chans * block + (q + 1) * half)
            work[at, re_l] = jnp.where(line_of == c, folded(gr * hr + gi * hi_), work[at, re_l])
            work[at, im_l] = jnp.where(line_of == c, folded(gr * hi_ - gi * hr), work[at, im_l])

    multiply(work, chans * block, block, tables_ref, 2)
    for m, (re, im) in enumerate(load_inverse(work, chans * block)):
        outgoing[m] = re

    def sum_copy(o, slot, target):
        return pltpu.make_async_remote_copy(
            src_ref=outgoing.at[target % outer], dst_ref=incoming.at[slot],
            send_sem=sum_send.at[o], recv_sem=sum_recv.at[slot],
            device_id=place(target), device_id_type=MESH)

    @pl.loop(1, n)
    def _(o):
        sum_copy(o, me, (me + o) % n).start()

    incoming[me] = outgoing[me % outer]
    partial[...] = jnp.zeros(partial.shape, jnp.float32)

    @pl.loop(0, chans)
    def _(c):
        sums = [jnp.zeros((half, LANES), jnp.float32) for _ in range(10)]
        for m in range(outer):
            for rows in (lo, hi):
                grad = back[c, rows, cols(m)] * slope[c, rows, cols(m)]
                for t in range(9):
                    sums[t] = sums[t] + grad * proj_shift[t, rows, cols(m)]
                sums[9] = sums[9] + grad
        for t in range(10):
            partial[c, t : t + 1, :] = folded(sums[t])

    for s in range(0, chans * block, step):
        multiply(work, s, step, tables_ref, 2)

    @pl.loop(0, chans)
    def _(c):
        sums = [jnp.zeros((half, LANES), jnp.float32) for _ in range(9)]
        for m, (re, im) in enumerate(load_inverse(work, start_of(c))):
            filt[c, lo, cols(m)] = re
            filt[c, hi, cols(m)] = im
            for t in range(9):
                sums[t] = sums[t] + re * cot_shift[t, lo, cols(m)] + im * cot_shift[t, hi, cols(m)]
        for t in range(9):
            partial[c, 16 + t : 17 + t, :] = folded(sums[t])

    small = lax.dot_general(
        jnp.ones((8, LANES), jnp.float32), partial[...].reshape(chans * SLOTS, LANES),
        (((1,), (1,)), ((), ())),
        precision=lax.Precision.HIGHEST, preferred_element_type=jnp.float32)
    width = chans_dev * SLOTS
    for h in range(ch_n):
        small_own[h] = small[0:1, h * width : (h + 1) * width]

    def small_copy(o, slot, target):
        return pltpu.make_async_remote_copy(
            src_ref=small_own.at[target % ch_n], dst_ref=small_in.at[slot],
            send_sem=small_send.at[o], recv_sem=small_recv.at[slot],
            device_id=place(target), device_id_type=MESH)

    @pl.loop(1, n)
    def _(o):
        small_copy(o, me, (me + o) % n).start()

    small_in[me] = small_own[c0]

    @pl.loop(1, n)
    def _(o):
        source = (me + o) % n
        sum_copy(o, source, source).wait_recv()

    total = incoming[0]
    for d in range(1, n):
        total = total + incoming[d]
    mine = me % outer
    group = me - mine
    collected[mine] = total

    def gather_copy(o, slot, target):
        return pltpu.make_async_remote_copy(
            src_ref=collected.at[mine], dst_ref=collected.at[slot],
            send_sem=gather_send.at[o], recv_sem=gather_recv.at[slot],
            device_id=place(group + target), device_id_type=MESH)

    @pl.loop(1, outer)
    def _(o):
        gather_copy(o, mine, (mine + o) % outer).start()

    @pl.loop(0, outer)
    def _(m):
        at = pl.ds(pl.multiple_of(m * LANES, LANES), LANES)
        for rows in (lo, hi):
            pieces = [filt[c, rows, at] for c in range(chans)]
            for t in range(9):
                total = second_ref[t // 3, t % 3, 0] * pieces[0]
                for c in range(1, chans):
                    total = total + second_ref[t // 3, t % 3, c] * pieces[c]
                mixed[t, rows, at] = total

    sides = []
    for j in range(3):
        total = mixed[3 + j]
        for i in (0, 2):
            total = total + pltpu.roll(mixed[3 * i + j], -(i - 1) * rq % both, 0)
        sides.append(total)
    image = sides[1] + from_left(sides[0]) + from_right(sides[2])
    for a in range(angles):
        sino_ref[a] = image[a * rq : (a + 1) * rq]

    @pl.loop(1, n)
    def _(o):
        source = (me + o) % n
        small_copy(o, source, source).wait_recv()

    sums = small_in[0]
    for d in range(1, n):
        sums = sums + small_in[d]
    for l in range(chans_dev):
        for i in range(3):
            at = l * SLOTS + 3 * i
            first_out_ref[i, l : l + 1, :] = sums[:, at : at + 3]
            second_out_ref[i, l : l + 1, :] = sums[:, at + 16 : at + 19]
        bias_out_ref[0:1, l : l + 1] = sums[:, l * SLOTS + 9 : l * SLOTS + 10]

    @pl.loop(1, outer)
    def _(o):
        source = (mine + o) % outer
        gather_copy(o, source, source).wait_recv()

    for m in range(outer):
        taps_out_ref[:, cols(m)] = collected[m, pl.ds(c0 * chans_dev, chans_dev), :]

    for o in range(1, ang_n):
        rows_copy(o, z, (z + o) % ang_n).wait_send()
    for o in range(1, ch_n):
        taps_copy(o, c0, (c0 + o) % ch_n).wait_send()
        packed_copy(o, c0, (c0 + o) % ch_n).wait_send()

    @pl.when(sends_top)
    def _():
        top_copy(z).wait_send()

    @pl.when(sends_bottom)
    def _():
        bottom_copy(z).wait_send()

    @pl.loop(1, n)
    def _(o):
        sum_copy(o, me, (me + o) % n).wait_send()
        small_copy(o, me, (me + o) % n).wait_send()

    @pl.loop(1, outer)
    def _(o):
        gather_copy(o, mine, (mine + o) % outer).wait_send()


def deliver(*refs):
    count = len(refs) // 2
    sems = refs[-1]
    copies = [
        pltpu.make_async_copy(refs[at], refs[count + at], sems.at[at]) for at in range(count)
    ]
    for copy in copies:
        copy.start()
    for copy in copies:
        copy.wait()


def on_device(sizes, tables, projections, conv1_weight, conv1_bias, filter_taps, conv2_weight, cotangent):
    ang_n, row_n, ch_n = sizes
    n = ang_n * row_n * ch_n
    _, held, columns = projections.shape
    chans_dev = conv1_weight.shape[0]
    chans = chans_dev * ch_n
    _, angles, rq, _ = cotangent.shape
    outer = columns // LANES
    both = angles * rq
    block = outer * both // 2
    f32 = jnp.float32
    vmem = pl.BlockSpec(memory_space=pltpu.VMEM)
    hbm = pl.BlockSpec(memory_space=pltpu.HBM)
    dma = pltpu.SemaphoreType.DMA
    wide = (both, columns)
    shapes = (
        jax.ShapeDtypeStruct((angles, rq, columns), f32),
        jax.ShapeDtypeStruct((3, chans_dev, 3), f32),
        jax.ShapeDtypeStruct((1, chans_dev), f32),
        jax.ShapeDtypeStruct((chans_dev, columns), f32),
        jax.ShapeDtypeStruct((3, chans_dev, 3), f32),
    )
    results = pl.pallas_call(
        functools.partial(kernel, sizes),
        out_shape=shapes,
        in_specs=[hbm] * 4 + [pl.BlockSpec(memory_space=pltpu.SMEM)] + [hbm] * 3,
        out_specs=(vmem,) * 5,
        scratch_shapes=[
            pltpu.VMEM((held, columns), f32),
            pltpu.VMEM((3, chans_dev, 3), f32),
            pltpu.VMEM((1, chans_dev), f32),
            pltpu.VMEM((chans_dev, columns), f32),
            pltpu.VMEM((angles, rq, columns), f32),
            pltpu.VMEM(tables[0].shape, jnp.bfloat16),
            pltpu.VMEM(tables[1].shape, f32),
            pltpu.VMEM(((held + 2) * outer, LANES), f32),
            pltpu.VMEM((chans_dev, LANES), f32),
            pltpu.VMEM((n, 1, LANES), f32),
            pltpu.VMEM((ch_n, 1, LANES), f32),
            pltpu.VMEM((ang_n, (rq + 2) * outer, LANES), f32),
            pltpu.VMEM((ang_n, outer, LANES), f32),
            pltpu.VMEM((ang_n, outer, LANES), f32),
            pltpu.VMEM((ch_n, chans_dev, columns), f32),
            pltpu.VMEM((ch_n, chans_dev, LANES), f32),
            pltpu.SMEM((ch_n, chans_dev, LANES), f32),
            pltpu.VMEM((9,) + wide, f32),
            pltpu.VMEM((9,) + wide, f32),
            pltpu.VMEM((chans * block, 2 * LANES), f32),
            pltpu.VMEM((chans * block, 2 * LANES), f32),
            pltpu.VMEM((block, 2 * LANES), f32),
            pltpu.VMEM(((chans + 1) * block, 2 * LANES), f32),
            pltpu.VMEM((chans,) + wide, f32),
            pltpu.VMEM((chans,) + wide, f32),
            pltpu.VMEM((chans,) + wide, f32),
            pltpu.VMEM((chans, SLOTS, LANES), f32),
            pltpu.VMEM((9,) + wide, f32),
            pltpu.VMEM((outer, chans, LANES), f32),
            pltpu.VMEM((n, chans, LANES), f32),
            pltpu.VMEM((outer, chans, LANES), f32),
            dma((ang_n,)), dma((ang_n,)), dma((2,)), dma((2, ang_n)),
            dma((ch_n,)), dma((ch_n,)), dma((ch_n,)), dma((ch_n,)),
            dma((n,)), dma((n,)), dma((outer,)), dma((outer,)),
            dma((n,)), dma((n,)), dma((7,)), dma(()),
        ],
        compiler_params=pltpu.CompilerParams(
            collective_id=0, has_side_effects=True, vmem_limit_bytes=63 * 2**20
        ),
        name="tomography",
    )(
        projections[0], jnp.transpose(conv1_weight, (1, 0, 2)), conv1_bias[None], filter_taps,
        jnp.transpose(conv2_weight, (1, 2, 0)), cotangent[0], *tables,
    )
    image, first, bias, taps_out, second = pl.pallas_call(
        deliver,
        out_shape=shapes,
        in_specs=[hbm] * 5,
        out_specs=(hbm,) * 5,
        scratch_shapes=[dma((5,))],
        compiler_params=pltpu.CompilerParams(vmem_limit_bytes=63 * 2**20),
        name="deliver",
    )(*results)
    return (
        image[None], jnp.transpose(first, (1, 0, 2)), bias[0], taps_out,
        jnp.transpose(second, (1, 0, 2)),
    )


def solution(mesh):
    sizes = tuple(mesh.shape[axis] for axis in ("ang", "row", "ch"))

    def whole(projections, conv1_weight, conv1_bias, filter_taps, conv2_weight, cotangent):
        tables = make_tables(projections.shape[-1])

        def local(*arrays):
            return on_device(sizes, tuple(jnp.asarray(t) for t in tables), *arrays)

        return jax.shard_map(
            local,
            mesh=mesh,
            in_specs=(
                P(("slab", "ang"), "row", None),
                P("ch", None, None),
                P("ch"),
                P("ch", None),
                P(),
                P(("slab", "row"), None, ("ang", "ch"), None),
            ),
            out_specs=(
                P(("slab", "row"), None, ("ang", "ch"), None),
                P(("slab", "ch"), None, None),
                P(("slab", "ch")),
                P(("slab", "ch"), None),
                P(("slab", "ch"), None, None),
            ),
            check_vma=False,
        )(projections, conv1_weight, conv1_bias, filter_taps, conv2_weight, cotangent)

    return whole
```

```python
import functools
import math

import jax
import jax.numpy as jnp
import numpy as np
import ml_dtypes
from jax import lax
from jax.experimental import pallas as pl
from jax.experimental.pallas import tpu as pltpu
from jax.sharding import PartitionSpec as P

MESH = pl.DeviceIdType.MESH
LANES = 128
SLOTS = 32


def twisted(value, k, n, sign):
    re, im = value
    if k == 0:
        return value
    if 4 * k == n:
        return (-im, re) if sign > 0 else (im, -re)
    if 8 * k == n:
        half = math.sqrt(0.5)
        return (half * (re - sign * im), half * (im + sign * re))
    if 8 * k == 3 * n:
        half = math.sqrt(0.5)
        return (half * (-re - sign * im), half * (-im + sign * re))
    cos = math.cos(2 * math.pi * k / n)
    sin = sign * math.sin(2 * math.pi * k / n)
    return (cos * re - sin * im, cos * im + sin * re)


def short_dft(values, sign):
    n = len(values)
    if n == 1:
        return values
    even = short_dft(values[0::2], sign)
    odd = short_dft(values[1::2], sign)
    low, high = [], []
    for k in range(n // 2):
        re, im = twisted(odd[k], k, n, sign)
        low.append((even[k][0] + re, even[k][1] + im))
        high.append((even[k][0] - re, even[k][1] - im))
    return low + high


def split_high_low(table):
    high = table.astype(ml_dtypes.bfloat16)
    low = (table - high.astype(np.float64)).astype(ml_dtypes.bfloat16)
    return high, low


def make_tables(length):
    outer = length // LANES
    index = np.arange(LANES)
    inner = 2 * np.pi * (np.outer(index, index) % LANES) / LANES
    cos, sin = np.cos(inner), np.sin(inner)
    forward = np.block([[cos, -sin], [sin, cos]])
    inverse = np.block([[cos, sin], [-sin, cos]]) / length
    twist = 2 * np.pi * np.outer(np.arange(outer), index) / length
    twist = np.repeat(twist, 8, axis=0)
    tables = np.stack([*split_high_low(forward), *split_high_low(inverse)])
    turns = np.stack([np.cos(twist), np.sin(twist)]).astype(np.float32)
    return tables, turns


def multiply(ref, start, rows, tables_ref, which):
    values = ref[pl.ds(start, rows), :]
    high = values.astype(jnp.bfloat16)
    low = (values - high.astype(jnp.float32)).astype(jnp.bfloat16)
    dot = functools.partial(jnp.dot, preferred_element_type=jnp.float32)
    table_high = tables_ref[which]
    ref[pl.ds(start, rows), :] = (
        dot(high, table_high) + dot(low, table_high) + dot(high, tables_ref[which + 1])
    )


def kernel(
    sizes,
    proj_hbm, first_hbm, bias_hbm, taps_hbm, second_ref, cot_hbm, tables_hbm, turns_hbm,
    sino_ref, first_out_ref, bias_out_ref, taps_out_ref, second_out_ref,
    proj_ref, first_vmem, bias_vmem, taps_ref, cot_ref, tables_ref, turns_ref,
    rows_ref, packed_ref, small_in, small_own,
    got, top, bottom, all_taps, all_packed, first_ref,
    cot_shift, proj_shift, spec_back, spec_hidden, spec_taps, work,
    back, slope, filt, partial, mixed,
    outgoing, incoming, collected,
    rows_send, rows_recv, edge_send, edge_recv, taps_send, taps_recv,
    packed_send, packed_recv, sum_send, sum_recv, gather_send, gather_recv, small_send, small_recv, load_sem, local_sem,
):
    ang_n, row_n, ch_n = sizes
    n = ang_n * row_n * ch_n
    angles, rq, columns = cot_ref.shape
    chans = second_ref.shape[2]
    chans_dev = taps_ref.shape[0]
    held = proj_ref.shape[0]
    both = angles * rq
    half = both // 2
    outer = columns // LANES
    block = outer * half
    slab = lax.axis_index("slab")
    z, k, c0 = lax.axis_index("ang"), lax.axis_index("row"), lax.axis_index("ch")
    me = (z * row_n + k) * ch_n + c0

    def place(d):
        return (slab, d // (row_n * ch_n), d // ch_n % row_n, d % ch_n)

    barrier = pltpu.get_barrier_semaphore()

    @pl.loop(1, n)
    def _(o):
        pl.semaphore_signal(barrier, inc=1, device_id=place((me + o) % n), device_id_type=MESH)

    loads = [
        pltpu.make_async_copy(source, target, load_sem.at[at])
        for at, (source, target) in enumerate((
            (proj_hbm, proj_ref), (first_hbm, first_vmem), (bias_hbm, bias_vmem),
            (taps_hbm, taps_ref), (cot_hbm, cot_ref), (tables_hbm, tables_ref),
            (turns_hbm, turns_ref)))
    ]
    for load in loads:
        load.start()

    def cols(m):
        return slice(m * LANES, (m + 1) * LANES)

    edge = jnp.zeros((outer, LANES), jnp.float32)
    rows_ref[0:outer, :] = edge
    rows_ref[(held + 1) * outer : (held + 2) * outer, :] = edge
    packed_ref[...] = jnp.zeros(packed_ref.shape, jnp.float32)
    loads[0].wait()
    for at in range(0, held, 8):
        for m in range(outer):
            rows_ref[pl.ds((at + 1) * outer + m, 8, stride=outer), :] = proj_ref[at : at + 8, cols(m)]
    loads[1].wait()
    loads[2].wait()
    for i in range(3):
        packed_ref[:, 3 * i : 3 * i + 3] = first_vmem[i]
    for l in range(chans_dev):
        packed_ref[l : l + 1, 9:10] = bias_vmem[0:1, l : l + 1]
    loads[3].wait()
    pl.semaphore_wait(barrier, n - 1)

    def rows_copy(o, slot, target):
        start = pl.multiple_of((target * ch_n + c0) * rq * outer, outer)
        return pltpu.make_async_remote_copy(
            src_ref=rows_ref.at[pl.ds(start, (rq + 2) * outer)], dst_ref=got.at[slot],
            send_sem=rows_send.at[o], recv_sem=rows_recv.at[slot],
            device_id=(slab, target, k, c0), device_id_type=MESH)

    def taps_copy(o, slot, target):
        return pltpu.make_async_remote_copy(
            src_ref=taps_ref, dst_ref=all_taps.at[slot],
            send_sem=taps_send.at[o], recv_sem=taps_recv.at[slot],
            device_id=(slab, z, k, target), device_id_type=MESH)

    def packed_copy(o, slot, target):
        return pltpu.make_async_remote_copy(
            src_ref=packed_ref, dst_ref=all_packed.at[slot],
            send_sem=packed_send.at[o], recv_sem=packed_recv.at[slot],
            device_id=(slab, z, k, target), device_id_type=MESH)

    def top_copy(slot):
        return pltpu.make_async_remote_copy(
            src_ref=rows_ref.at[pl.ds(held * outer, outer)], dst_ref=top.at[slot],
            send_sem=edge_send.at[0], recv_sem=edge_recv.at[0, slot],
            device_id=(slab, 0, (k + 1) % row_n, 0), device_id_type=MESH)

    def bottom_copy(slot):
        return pltpu.make_async_remote_copy(
            src_ref=rows_ref.at[pl.ds(outer, outer)], dst_ref=bottom.at[slot],
            send_sem=edge_send.at[1], recv_sem=edge_recv.at[1, slot],
            device_id=(slab, ang_n - 1, (k + row_n - 1) % row_n, ch_n - 1), device_id_type=MESH)

    for o in range(1, ch_n):
        taps_copy(o, c0, (c0 + o) % ch_n).start()
        packed_copy(o, c0, (c0 + o) % ch_n).start()
    sends_top = jnp.logical_and(c0 == 0, k < row_n - 1)
    sends_bottom = jnp.logical_and(c0 == ch_n - 1, k > 0)

    @pl.when(sends_top)
    def _():
        top_copy(z).start()

    @pl.when(sends_bottom)
    def _():
        bottom_copy(z).start()

    for o in range(1, ang_n):
        rows_copy(o, z, (z + o) % ang_n).start()

    mine_at = pl.multiple_of((z * ch_n + c0) * rq * outer, outer)
    got[z] = rows_ref[pl.ds(mine_at, (rq + 2) * outer), :]
    all_taps[c0] = taps_ref[...]
    all_packed[c0] = packed_ref[...]

    column = lax.broadcasted_iota(jnp.int32, (both, columns), 1)
    first_col, last_col = column == 0, column == columns - 1

    def from_left(x):
        return jnp.where(first_col, 0.0, pltpu.roll(x, 1, 1))

    def from_right(x):
        return jnp.where(last_col, 0.0, pltpu.roll(x, columns - 1, 1))

    lo, hi = slice(0, half), slice(half, both)
    re_l, im_l = slice(0, LANES), slice(LANES, 2 * LANES)

    loads[4].wait()
    upstream = jnp.concatenate([cot_ref[a] for a in range(angles)], axis=0)
    for i in range(3):
        shift = (i - 1) * rq % both
        turned = pltpu.roll(upstream, shift, 0) if shift else upstream
        cot_shift[3 * i] = from_right(turned)
        cot_shift[3 * i + 1] = turned
        cot_shift[3 * i + 2] = from_left(turned)

    def store_forward(ref, start, values):
        for q, (re, im) in enumerate(short_dft(values, -1)):
            part = slice(q * half, (q + 1) * half)
            cos, sin = turns_ref[0, part, :], turns_ref[1, part, :]
            rows = pl.ds(start + q * half, half)
            ref[rows, re_l] = re * cos + im * sin
            ref[rows, im_l] = im * cos - re * sin

    def load_inverse(ref, start):
        values = []
        for q in range(outer):
            part = slice(q * half, (q + 1) * half)
            cos, sin = turns_ref[0, part, :], turns_ref[1, part, :]
            rows = pl.ds(start + q * half, half)
            re, im = ref[rows, re_l], ref[rows, im_l]
            values.append((re * cos - im * sin, im * cos + re * sin))
        return short_dft(values, 1)

    def start_of(c):
        return pl.multiple_of(c * block, block)

    loads[5].wait()
    loads[6].wait()

    @pl.loop(0, chans)
    def _(c):
        weights = [second_ref[t // 3, t % 3, c] for t in range(9)]
        values = []
        for m in range(outer):
            pair = []
            for rows in (lo, hi):
                total = weights[0] * cot_shift[0, rows, cols(m)]
                for t in range(1, 9):
                    total = total + weights[t] * cot_shift[t, rows, cols(m)]
                pair.append(total)
            values.append(tuple(pair))
        store_forward(spec_back, start_of(c), values)

    step = 4 * block
    for s in range(0, chans * block, step):
        multiply(spec_back, s, step, tables_ref, 0)

    for o in range(1, ch_n):
        source = (c0 + o) % ch_n
        taps_copy(o, source, source).wait_recv()
        packed_copy(o, source, source).wait_recv()
    load_weights = pltpu.make_async_copy(all_packed, first_ref, local_sem)
    load_weights.start()
    taps = jnp.concatenate([all_taps[h] for h in range(ch_n)], axis=0)
    zero = jnp.zeros((chans, LANES), jnp.float32)
    store_forward(spec_taps, 0, [(taps[:, cols(m)], zero) for m in range(outer)])
    multiply(spec_taps, 0, block, tables_ref, 0)

    def tap_row(q, c):
        row = spec_taps[pl.ds(q * half + c, 1), :]
        row = jnp.broadcast_to(row, (half, 2 * LANES))
        return row[:, re_l], row[:, im_l]

    @pl.loop(0, chans)
    def _(c):
        for q in range(outer):
            tr, ti = tap_row(q, c)
            rows = pl.ds(start_of(c) + q * half, half)
            gr, gi = spec_back[rows, re_l], spec_back[rows, im_l]
            work[rows, re_l] = tr * gr - ti * gi
            work[rows, im_l] = tr * gi + ti * gr

    for s in range(0, chans * block, step):
        multiply(work, s, step, tables_ref, 2)

    @pl.loop(0, chans)
    def _(c):
        for m, (re, im) in enumerate(load_inverse(work, start_of(c))):
            back[c, lo, cols(m)] = re
            back[c, hi, cols(m)] = im

    load_weights.wait()
    for o in range(1, ang_n):
        source = (z + o) % ang_n
        rows_copy(o, source, source).wait_recv()

    @pl.when(jnp.logical_and(jnp.logical_and(z == 0, c0 == 0), k > 0))
    def _():
        for a in range(ang_n):
            top_copy(a).wait_recv()
            got[a, 0:outer, :] = top[a]

    @pl.when(jnp.logical_and(jnp.logical_and(z == ang_n - 1, c0 == ch_n - 1), k < row_n - 1))
    def _():
        for a in range(ang_n):
            bottom_copy(a).wait_recv()
            got[a, (rq + 1) * outer : (rq + 2) * outer, :] = bottom[a]

    for a in range(angles):
        for i in range(3):
            for m in range(outer):
                lines = got[a, pl.ds(i * outer + m, rq, stride=outer), :]
                proj_shift[3 * i + 1, a * rq : (a + 1) * rq, cols(m)] = lines
    for i in range(3):
        centre = proj_shift[3 * i + 1]
        proj_shift[3 * i] = from_left(centre)
        proj_shift[3 * i + 2] = from_right(centre)

    @pl.loop(0, chans)
    def _(c):
        h, l = c // chans_dev, c % chans_dev
        weights = [first_ref[h, l, t] for t in range(10)]
        values = []
        for m in range(outer):
            pair = []
            for rows in (lo, hi):
                pre = weights[9] + weights[0] * proj_shift[0, rows, cols(m)]
                for t in range(1, 9):
                    pre = pre + weights[t] * proj_shift[t, rows, cols(m)]
                gate = 0.5 + 0.5 * jnp.tanh(0.5 * pre)
                slope[c, rows, cols(m)] = gate * (1.0 + pre * (1.0 - gate))
                pair.append(pre * gate)
            values.append(tuple(pair))
        store_forward(spec_hidden, start_of(c), values)

    for s in range(0, chans * block, step):
        multiply(spec_hidden, s, step, tables_ref, 0)
    work[pl.ds(chans * block, block), :] = jnp.zeros((block, 2 * LANES), jnp.float32)
    line_of = lax.broadcasted_iota(jnp.int32, (half, LANES), 0)

    def folded(value):
        return jnp.sum(value, axis=0, keepdims=True)


    @pl.loop(0, chans)
    def _(c):
        for q in range(outer):
            tr, ti = tap_row(q, c)
            rows = pl.ds(start_of(c) + q * half, half)
            gr, gi = spec_back[rows, re_l], spec_back[rows, im_l]
            hr, hi_ = spec_hidden[rows, re_l], spec_hidden[rows, im_l]
            work[rows, re_l] = tr * hr + ti * hi_
            work[rows, im_l] = tr * hi_ - ti * hr
            at = slice(chans * block + q * half, chans * block + (q + 1) * half)
            work[at, re_l] = jnp.where(line_of == c, folded(gr * hr + gi * hi_), work[at, re_l])
            work[at, im_l] = jnp.where(line_of == c, folded(gr * hi_ - gi * hr), work[at, im_l])

    multiply(work, chans * block, block, tables_ref, 2)
    for m, (re, im) in enumerate(load_inverse(work, chans * block)):
        outgoing[m] = re

    def sum_copy(o, slot, target):
        return pltpu.make_async_remote_copy(
            src_ref=outgoing.at[target % outer], dst_ref=incoming.at[slot],
            send_sem=sum_send.at[o], recv_sem=sum_recv.at[slot],
            device_id=place(target), device_id_type=MESH)

    @pl.loop(1, n)
    def _(o):
        sum_copy(o, me, (me + o) % n).start()

    incoming[me] = outgoing[me % outer]
    partial[...] = jnp.zeros(partial.shape, jnp.float32)

    @pl.loop(0, chans)
    def _(c):
        sums = [jnp.zeros((half, LANES), jnp.float32) for _ in range(10)]
        for m in range(outer):
            for rows in (lo, hi):
                grad = back[c, rows, cols(m)] * slope[c, rows, cols(m)]
                for t in range(9):
                    sums[t] = sums[t] + grad * proj_shift[t, rows, cols(m)]
                sums[9] = sums[9] + grad
        for t in range(10):
            partial[c, t : t + 1, :] = folded(sums[t])

    for s in range(0, chans * block, step):
        multiply(work, s, step, tables_ref, 2)

    @pl.loop(0, chans)
    def _(c):
        sums = [jnp.zeros((half, LANES), jnp.float32) for _ in range(9)]
        for m, (re, im) in enumerate(load_inverse(work, start_of(c))):
            filt[c, lo, cols(m)] = re
            filt[c, hi, cols(m)] = im
            for t in range(9):
                sums[t] = sums[t] + re * cot_shift[t, lo, cols(m)] + im * cot_shift[t, hi, cols(m)]
        for t in range(9):
            partial[c, 16 + t : 17 + t, :] = folded(sums[t])

    small = lax.dot_general(
        jnp.ones((8, LANES), jnp.float32), partial[...].reshape(chans * SLOTS, LANES),
        (((1,), (1,)), ((), ())),
        precision=lax.Precision.HIGHEST, preferred_element_type=jnp.float32)
    width = chans_dev * SLOTS
    for h in range(ch_n):
        small_own[h] = small[0:1, h * width : (h + 1) * width]

    def small_copy(o, slot, target):
        return pltpu.make_async_remote_copy(
            src_ref=small_own.at[target % ch_n], dst_ref=small_in.at[slot],
            send_sem=small_send.at[o], recv_sem=small_recv.at[slot],
            device_id=place(target), device_id_type=MESH)

    @pl.loop(1, n)
    def _(o):
        small_copy(o, me, (me + o) % n).start()

    small_in[me] = small_own[c0]

    @pl.loop(1, n)
    def _(o):
        source = (me + o) % n
        sum_copy(o, source, source).wait_recv()

    total = incoming[0]
    for d in range(1, n):
        total = total + incoming[d]
    mine = me % outer
    group = me - mine
    collected[mine] = total

    def gather_copy(o, slot, target):
        return pltpu.make_async_remote_copy(
            src_ref=collected.at[mine], dst_ref=collected.at[slot],
            send_sem=gather_send.at[o], recv_sem=gather_recv.at[slot],
            device_id=place(group + target), device_id_type=MESH)

    @pl.loop(1, outer)
    def _(o):
        gather_copy(o, mine, (mine + o) % outer).start()

    @pl.loop(0, outer)
    def _(m):
        at = pl.ds(pl.multiple_of(m * LANES, LANES), LANES)
        for rows in (lo, hi):
            pieces = [filt[c, rows, at] for c in range(chans)]
            for t in range(9):
                total = second_ref[t // 3, t % 3, 0] * pieces[0]
                for c in range(1, chans):
                    total = total + second_ref[t // 3, t % 3, c] * pieces[c]
                mixed[t, rows, at] = total

    sides = []
    for j in range(3):
        total = mixed[3 + j]
        for i in (0, 2):
            total = total + pltpu.roll(mixed[3 * i + j], -(i - 1) * rq % both, 0)
        sides.append(total)
    image = sides[1] + from_left(sides[0]) + from_right(sides[2])
    for a in range(angles):
        sino_ref[a] = image[a * rq : (a + 1) * rq]

    @pl.loop(1, n)
    def _(o):
        source = (me + o) % n
        small_copy(o, source, source).wait_recv()

    sums = small_in[0]
    for d in range(1, n):
        sums = sums + small_in[d]
    for l in range(chans_dev):
        for i in range(3):
            at = l * SLOTS + 3 * i
            first_out_ref[i, l : l + 1, :] = sums[:, at : at + 3]
            second_out_ref[i, l : l + 1, :] = sums[:, at + 16 : at + 19]
        bias_out_ref[0:1, l : l + 1] = sums[:, l * SLOTS + 9 : l * SLOTS + 10]

    @pl.loop(1, outer)
    def _(o):
        source = (mine + o) % outer
        gather_copy(o, source, source).wait_recv()

    for m in range(outer):
        taps_out_ref[:, cols(m)] = collected[m, pl.ds(c0 * chans_dev, chans_dev), :]

    for o in range(1, ang_n):
        rows_copy(o, z, (z + o) % ang_n).wait_send()
    for o in range(1, ch_n):
        taps_copy(o, c0, (c0 + o) % ch_n).wait_send()
        packed_copy(o, c0, (c0 + o) % ch_n).wait_send()

    @pl.when(sends_top)
    def _():
        top_copy(z).wait_send()

    @pl.when(sends_bottom)
    def _():
        bottom_copy(z).wait_send()

    @pl.loop(1, n)
    def _(o):
        sum_copy(o, me, (me + o) % n).wait_send()
        small_copy(o, me, (me + o) % n).wait_send()

    @pl.loop(1, outer)
    def _(o):
        gather_copy(o, mine, (mine + o) % outer).wait_send()


def deliver(*refs):
    count = (len(refs) - 1) // 3
    sources, targets, staged = refs[:count], refs[count : 2 * count], refs[2 * count : 3 * count]
    sems = refs[-1]
    into = [pltpu.make_async_copy(sources[at], staged[at], sems.at[0, at]) for at in range(count)]
    out = [pltpu.make_async_copy(staged[at], targets[at], sems.at[1, at]) for at in range(count)]
    for copy in into:
        copy.start()
    for copy_in, copy_out in zip(into, out):
        copy_in.wait()
        copy_out.start()
    for copy in out:
        copy.wait()


def on_device(sizes, tables, projections, conv1_weight, conv1_bias, filter_taps, conv2_weight, cotangent):
    ang_n, row_n, ch_n = sizes
    n = ang_n * row_n * ch_n
    _, held, columns = projections.shape
    chans_dev = conv1_weight.shape[0]
    chans = chans_dev * ch_n
    _, angles, rq, _ = cotangent.shape
    outer = columns // LANES
    both = angles * rq
    block = outer * both // 2
    f32 = jnp.float32
    vmem = pl.BlockSpec(memory_space=pltpu.VMEM)
    hbm = pl.BlockSpec(memory_space=pltpu.HBM)
    dma = pltpu.SemaphoreType.DMA
    wide = (both, columns)
    shapes = (
        jax.ShapeDtypeStruct((angles, rq, columns), f32),
        jax.ShapeDtypeStruct((3, chans_dev, 3), f32),
        jax.ShapeDtypeStruct((1, chans_dev), f32),
        jax.ShapeDtypeStruct((chans_dev, columns), f32),
        jax.ShapeDtypeStruct((3, chans_dev, 3), f32),
    )
    results = pl.pallas_call(
        functools.partial(kernel, sizes),
        out_shape=shapes,
        in_specs=[hbm] * 4 + [pl.BlockSpec(memory_space=pltpu.SMEM)] + [hbm] * 3,
        out_specs=(vmem,) * 5,
        scratch_shapes=[
            pltpu.VMEM((held, columns), f32),
            pltpu.VMEM((3, chans_dev, 3), f32),
            pltpu.VMEM((1, chans_dev), f32),
            pltpu.VMEM((chans_dev, columns), f32),
            pltpu.VMEM((angles, rq, columns), f32),
            pltpu.VMEM(tables[0].shape, jnp.bfloat16),
            pltpu.VMEM(tables[1].shape, f32),
            pltpu.VMEM(((held + 2) * outer, LANES), f32),
            pltpu.VMEM((chans_dev, LANES), f32),
            pltpu.VMEM((n, 1, LANES), f32),
            pltpu.VMEM((ch_n, 1, LANES), f32),
            pltpu.VMEM((ang_n, (rq + 2) * outer, LANES), f32),
            pltpu.VMEM((ang_n, outer, LANES), f32),
            pltpu.VMEM((ang_n, outer, LANES), f32),
            pltpu.VMEM((ch_n, chans_dev, columns), f32),
            pltpu.VMEM((ch_n, chans_dev, LANES), f32),
            pltpu.SMEM((ch_n, chans_dev, LANES), f32),
            pltpu.VMEM((9,) + wide, f32),
            pltpu.VMEM((9,) + wide, f32),
            pltpu.VMEM((chans * block, 2 * LANES), f32),
            pltpu.VMEM((chans * block, 2 * LANES), f32),
            pltpu.VMEM((block, 2 * LANES), f32),
            pltpu.VMEM(((chans + 1) * block, 2 * LANES), f32),
            pltpu.VMEM((chans,) + wide, f32),
            pltpu.VMEM((chans,) + wide, f32),
            pltpu.VMEM((chans,) + wide, f32),
            pltpu.VMEM((chans, SLOTS, LANES), f32),
            pltpu.VMEM((9,) + wide, f32),
            pltpu.VMEM((outer, chans, LANES), f32),
            pltpu.VMEM((n, chans, LANES), f32),
            pltpu.VMEM((outer, chans, LANES), f32),
            dma((ang_n,)), dma((ang_n,)), dma((2,)), dma((2, ang_n)),
            dma((ch_n,)), dma((ch_n,)), dma((ch_n,)), dma((ch_n,)),
            dma((n,)), dma((n,)), dma((outer,)), dma((outer,)),
            dma((n,)), dma((n,)), dma((7,)), dma(()),
        ],
        compiler_params=pltpu.CompilerParams(
            collective_id=0, has_side_effects=True, vmem_limit_bytes=63 * 2**20
        ),
        name="tomography",
    )(
        projections[0], jnp.transpose(conv1_weight, (1, 0, 2)), conv1_bias[None], filter_taps,
        jnp.transpose(conv2_weight, (1, 2, 0)), cotangent[0], *tables,
    )
    image, first, bias, taps_out, second = pl.pallas_call(
        deliver,
        out_shape=shapes,
        in_specs=[hbm] * 5,
        out_specs=(hbm,) * 5,
        scratch_shapes=[pltpu.VMEM(leaf.shape, f32) for leaf in shapes] + [dma((2, 5))],
        compiler_params=pltpu.CompilerParams(vmem_limit_bytes=63 * 2**20),
        name="deliver",
    )(*results)
    return (
        image[None], jnp.transpose(first, (1, 0, 2)), bias[0], taps_out,
        jnp.transpose(second, (1, 0, 2)),
    )


def solution(mesh):
    sizes = tuple(mesh.shape[axis] for axis in ("ang", "row", "ch"))

    def whole(projections, conv1_weight, conv1_bias, filter_taps, conv2_weight, cotangent):
        tables = make_tables(projections.shape[-1])

        def local(*arrays):
            return on_device(sizes, tuple(jnp.asarray(t) for t in tables), *arrays)

        return jax.shard_map(
            local,
            mesh=mesh,
            in_specs=(
                P(("slab", "ang"), "row", None),
                P("ch", None, None),
                P("ch"),
                P("ch", None),
                P(),
                P(("slab", "row"), None, ("ang", "ch"), None),
            ),
            out_specs=(
                P(("slab", "row"), None, ("ang", "ch"), None),
                P(("slab", "ch"), None, None),
                P(("slab", "ch")),
                P(("slab", "ch"), None),
                P(("slab", "ch"), None, None),
            ),
            check_vma=False,
        )(projections, conv1_weight, conv1_bias, filter_taps, conv2_weight, cotangent)

    return whole
```

```python
import functools
import math

import jax
import jax.numpy as jnp
import numpy as np
import ml_dtypes
from jax import lax
from jax.experimental import pallas as pl
from jax.experimental.pallas import tpu as pltpu
from jax.sharding import PartitionSpec as P

MESH = pl.DeviceIdType.MESH
LANES = 128
SLOTS = 32


def twisted(value, k, n, sign):
    re, im = value
    if k == 0:
        return value
    if 4 * k == n:
        return (-im, re) if sign > 0 else (im, -re)
    if 8 * k == n:
        half = math.sqrt(0.5)
        return (half * (re - sign * im), half * (im + sign * re))
    if 8 * k == 3 * n:
        half = math.sqrt(0.5)
        return (half * (-re - sign * im), half * (-im + sign * re))
    cos = math.cos(2 * math.pi * k / n)
    sin = sign * math.sin(2 * math.pi * k / n)
    return (cos * re - sin * im, cos * im + sin * re)


def short_dft(values, sign):
    n = len(values)
    if n == 1:
        return values
    even = short_dft(values[0::2], sign)
    odd = short_dft(values[1::2], sign)
    low, high = [], []
    for k in range(n // 2):
        re, im = twisted(odd[k], k, n, sign)
        low.append((even[k][0] + re, even[k][1] + im))
        high.append((even[k][0] - re, even[k][1] - im))
    return low + high


def split_high_low(table):
    high = table.astype(ml_dtypes.bfloat16)
    low = (table - high.astype(np.float64)).astype(ml_dtypes.bfloat16)
    return high, low


def make_tables(length):
    outer = length // LANES
    index = np.arange(LANES)
    inner = 2 * np.pi * (np.outer(index, index) % LANES) / LANES
    cos, sin = np.cos(inner), np.sin(inner)
    forward = np.block([[cos, -sin], [sin, cos]])
    inverse = np.block([[cos, sin], [-sin, cos]]) / length
    twist = 2 * np.pi * np.outer(np.arange(outer), index) / length
    twist = np.repeat(twist, 8, axis=0)
    tables = np.stack([*split_high_low(forward), *split_high_low(inverse)])
    turns = np.stack([np.cos(twist), np.sin(twist)]).astype(np.float32)
    return tables, turns


def multiply(ref, start, rows, tables_ref, which):
    values = ref[pl.ds(start, rows), :]
    high = values.astype(jnp.bfloat16)
    low = (values - high.astype(jnp.float32)).astype(jnp.bfloat16)
    dot = functools.partial(jnp.dot, preferred_element_type=jnp.float32)
    table_high = tables_ref[which]
    ref[pl.ds(start, rows), :] = (
        dot(high, table_high) + dot(low, table_high) + dot(high, tables_ref[which + 1])
    )


def kernel(
    sizes,
    proj_hbm, first_hbm, bias_hbm, taps_hbm, second_ref, cot_hbm, tables_hbm, turns_hbm,
    sino_ref, first_out_ref, bias_out_ref, taps_out_ref, second_out_ref,
    proj_ref, first_vmem, bias_vmem, taps_ref, cot_ref, tables_ref, turns_ref,
    rows_ref, packed_ref, small_in, small_own,
    got, top, bottom, all_taps, all_packed, first_ref,
    cot_shift, proj_shift, spec_back, spec_hidden, spec_taps, work,
    back, slope, filt, partial, mixed,
    outgoing, incoming, collected,
    rows_send, rows_recv, edge_send, edge_recv, taps_send, taps_recv,
    packed_send, packed_recv, sum_send, sum_recv, gather_send, gather_recv, small_send, small_recv, load_sem, local_sem,
):
    ang_n, row_n, ch_n = sizes
    n = ang_n * row_n * ch_n
    angles, rq, columns = cot_ref.shape
    chans = second_ref.shape[2]
    chans_dev = taps_ref.shape[0]
    held = proj_ref.shape[0]
    both = angles * rq
    half = both // 2
    outer = columns // LANES
    block = outer * half
    slab = lax.axis_index("slab")
    z, k, c0 = lax.axis_index("ang"), lax.axis_index("row"), lax.axis_index("ch")
    me = (z * row_n + k) * ch_n + c0

    def place(d):
        return (slab, d // (row_n * ch_n), d // ch_n % row_n, d % ch_n)

    barrier = pltpu.get_barrier_semaphore()

    @pl.loop(1, n)
    def _(o):
        pl.semaphore_signal(barrier, inc=1, device_id=place((me + o) % n), device_id_type=MESH)

    loads = [
        pltpu.make_async_copy(source, target, load_sem.at[at])
        for at, (source, target) in enumerate((
            (proj_hbm, proj_ref), (first_hbm, first_vmem), (bias_hbm, bias_vmem),
            (taps_hbm, taps_ref), (cot_hbm, cot_ref), (tables_hbm, tables_ref),
            (turns_hbm, turns_ref)))
    ]
    for load in loads:
        load.start()

    def cols(m):
        return slice(m * LANES, (m + 1) * LANES)

    edge = jnp.zeros((outer, LANES), jnp.float32)
    rows_ref[0:outer, :] = edge
    rows_ref[(held + 1) * outer : (held + 2) * outer, :] = edge
    packed_ref[...] = jnp.zeros(packed_ref.shape, jnp.float32)
    loads[0].wait()
    for at in range(0, held, 8):
        for m in range(outer):
            rows_ref[pl.ds((at + 1) * outer + m, 8, stride=outer), :] = proj_ref[at : at + 8, cols(m)]
    loads[1].wait()
    loads[2].wait()
    for i in range(3):
        packed_ref[:, 3 * i : 3 * i + 3] = first_vmem[i]
    for l in range(chans_dev):
        packed_ref[l : l + 1, 9:10] = bias_vmem[0:1, l : l + 1]
    loads[3].wait()
    pl.semaphore_wait(barrier, n - 1)

    def rows_copy(o, slot, target):
        start = pl.multiple_of((target * ch_n + c0) * rq * outer, outer)
        return pltpu.make_async_remote_copy(
            src_ref=rows_ref.at[pl.ds(start, (rq + 2) * outer)], dst_ref=got.at[slot],
            send_sem=rows_send.at[o], recv_sem=rows_recv.at[slot],
            device_id=(slab, target, k, c0), device_id_type=MESH)

    def taps_copy(o, slot, target):
        return pltpu.make_async_remote_copy(
            src_ref=taps_ref, dst_ref=all_taps.at[slot],
            send_sem=taps_send.at[o], recv_sem=taps_recv.at[slot],
            device_id=(slab, z, k, target), device_id_type=MESH)

    def packed_copy(o, slot, target):
        return pltpu.make_async_remote_copy(
            src_ref=packed_ref, dst_ref=all_packed.at[slot],
            send_sem=packed_send.at[o], recv_sem=packed_recv.at[slot],
            device_id=(slab, z, k, target), device_id_type=MESH)

    def top_copy(slot):
        return pltpu.make_async_remote_copy(
            src_ref=rows_ref.at[pl.ds(held * outer, outer)], dst_ref=top.at[slot],
            send_sem=edge_send.at[0], recv_sem=edge_recv.at[0, slot],
            device_id=(slab, 0, (k + 1) % row_n, 0), device_id_type=MESH)

    def bottom_copy(slot):
        return pltpu.make_async_remote_copy(
            src_ref=rows_ref.at[pl.ds(outer, outer)], dst_ref=bottom.at[slot],
            send_sem=edge_send.at[1], recv_sem=edge_recv.at[1, slot],
            device_id=(slab, ang_n - 1, (k + row_n - 1) % row_n, ch_n - 1), device_id_type=MESH)

    for o in range(1, ang_n):
        rows_copy(o, z, (z + o) % ang_n).start()

    for o in range(1, ch_n):
        taps_copy(o, c0, (c0 + o) % ch_n).start()
        packed_copy(o, c0, (c0 + o) % ch_n).start()
    sends_top = jnp.logical_and(c0 == 0, k < row_n - 1)
    sends_bottom = jnp.logical_and(c0 == ch_n - 1, k > 0)

    @pl.when(sends_top)
    def _():
        top_copy(z).start()

    @pl.when(sends_bottom)
    def _():
        bottom_copy(z).start()

    mine_at = pl.multiple_of((z * ch_n + c0) * rq * outer, outer)
    got[z] = rows_ref[pl.ds(mine_at, (rq + 2) * outer), :]
    all_taps[c0] = taps_ref[...]
    all_packed[c0] = packed_ref[...]

    column = lax.broadcasted_iota(jnp.int32, (both, columns), 1)
    first_col, last_col = column == 0, column == columns - 1

    def from_left(x):
        return jnp.where(first_col, 0.0, pltpu.roll(x, 1, 1))

    def from_right(x):
        return jnp.where(last_col, 0.0, pltpu.roll(x, columns - 1, 1))

    lo, hi = slice(0, half), slice(half, both)
    re_l, im_l = slice(0, LANES), slice(LANES, 2 * LANES)

    loads[4].wait()
    upstream = jnp.concatenate([cot_ref[a] for a in range(angles)], axis=0)
    for i in range(3):
        shift = (i - 1) * rq % both
        turned = pltpu.roll(upstream, shift, 0) if shift else upstream
        cot_shift[3 * i] = from_right(turned)
        cot_shift[3 * i + 1] = turned
        cot_shift[3 * i + 2] = from_left(turned)

    def store_forward(ref, start, values):
        for q, (re, im) in enumerate(short_dft(values, -1)):
            part = slice(q * half, (q + 1) * half)
            cos, sin = turns_ref[0, part, :], turns_ref[1, part, :]
            rows = pl.ds(start + q * half, half)
            ref[rows, re_l] = re * cos + im * sin
            ref[rows, im_l] = im * cos - re * sin

    def load_inverse(ref, start):
        values = []
        for q in range(outer):
            part = slice(q * half, (q + 1) * half)
            cos, sin = turns_ref[0, part, :], turns_ref[1, part, :]
            rows = pl.ds(start + q * half, half)
            re, im = ref[rows, re_l], ref[rows, im_l]
            values.append((re * cos - im * sin, im * cos + re * sin))
        return short_dft(values, 1)

    def start_of(c):
        return pl.multiple_of(c * block, block)

    loads[5].wait()
    loads[6].wait()

    @pl.loop(0, chans)
    def _(c):
        weights = [second_ref[t // 3, t % 3, c] for t in range(9)]
        values = []
        for m in range(outer):
            pair = []
            for rows in (lo, hi):
                total = weights[0] * cot_shift[0, rows, cols(m)]
                for t in range(1, 9):
                    total = total + weights[t] * cot_shift[t, rows, cols(m)]
                pair.append(total)
            values.append(tuple(pair))
        store_forward(spec_back, start_of(c), values)

    step = 4 * block
    for s in range(0, chans * block, step):
        multiply(spec_back, s, step, tables_ref, 0)

    for o in range(1, ch_n):
        source = (c0 + o) % ch_n
        taps_copy(o, source, source).wait_recv()
        packed_copy(o, source, source).wait_recv()
    load_weights = pltpu.make_async_copy(all_packed, first_ref, local_sem)
    load_weights.start()
    taps = jnp.concatenate([all_taps[h] for h in range(ch_n)], axis=0)
    zero = jnp.zeros((chans, LANES), jnp.float32)
    store_forward(spec_taps, 0, [(taps[:, cols(m)], zero) for m in range(outer)])
    multiply(spec_taps, 0, block, tables_ref, 0)

    def tap_row(q, c):
        row = spec_taps[pl.ds(q * half + c, 1), :]
        row = jnp.broadcast_to(row, (half, 2 * LANES))
        return row[:, re_l], row[:, im_l]

    @pl.loop(0, chans)
    def _(c):
        for q in range(outer):
            tr, ti = tap_row(q, c)
            rows = pl.ds(start_of(c) + q * half, half)
            gr, gi = spec_back[rows, re_l], spec_back[rows, im_l]
            work[rows, re_l] = tr * gr - ti * gi
            work[rows, im_l] = tr * gi + ti * gr

    for s in range(0, chans * block, step):
        multiply(work, s, step, tables_ref, 2)

    @pl.loop(0, chans)
    def _(c):
        for m, (re, im) in enumerate(load_inverse(work, start_of(c))):
            back[c, lo, cols(m)] = re
            back[c, hi, cols(m)] = im

    load_weights.wait()
    for o in range(1, ang_n):
        source = (z + o) % ang_n
        rows_copy(o, source, source).wait_recv()

    @pl.when(jnp.logical_and(jnp.logical_and(z == 0, c0 == 0), k > 0))
    def _():
        for a in range(ang_n):
            top_copy(a).wait_recv()
            got[a, 0:outer, :] = top[a]

    @pl.when(jnp.logical_and(jnp.logical_and(z == ang_n - 1, c0 == ch_n - 1), k < row_n - 1))
    def _():
        for a in range(ang_n):
            bottom_copy(a).wait_recv()
            got[a, (rq + 1) * outer : (rq + 2) * outer, :] = bottom[a]

    for a in range(angles):
        for i in range(3):
            for m in range(outer):
                lines = got[a, pl.ds(i * outer + m, rq, stride=outer), :]
                proj_shift[3 * i + 1, a * rq : (a + 1) * rq, cols(m)] = lines
    for i in range(3):
        centre = proj_shift[3 * i + 1]
        proj_shift[3 * i] = from_left(centre)
        proj_shift[3 * i + 2] = from_right(centre)

    @pl.loop(0, chans)
    def _(c):
        h, l = c // chans_dev, c % chans_dev
        weights = [first_ref[h, l, t] for t in range(10)]
        values = []
        for m in range(outer):
            pair = []
            for rows in (lo, hi):
                pre = weights[9] + weights[0] * proj_shift[0, rows, cols(m)]
                for t in range(1, 9):
                    pre = pre + weights[t] * proj_shift[t, rows, cols(m)]
                gate = 0.5 + 0.5 * jnp.tanh(0.5 * pre)
                slope[c, rows, cols(m)] = gate * (1.0 + pre * (1.0 - gate))
                pair.append(pre * gate)
            values.append(tuple(pair))
        store_forward(spec_hidden, start_of(c), values)

    for s in range(0, chans * block, step):
        multiply(spec_hidden, s, step, tables_ref, 0)
    work[pl.ds(chans * block, block), :] = jnp.zeros((block, 2 * LANES), jnp.float32)
    line_of = lax.broadcasted_iota(jnp.int32, (half, LANES), 0)

    def folded(value):
        return jnp.sum(value, axis=0, keepdims=True)


    @pl.loop(0, chans)
    def _(c):
        for q in range(outer):
            tr, ti = tap_row(q, c)
            rows = pl.ds(start_of(c) + q * half, half)
            gr, gi = spec_back[rows, re_l], spec_back[rows, im_l]
            hr, hi_ = spec_hidden[rows, re_l], spec_hidden[rows, im_l]
            work[rows, re_l] = tr * hr + ti * hi_
            work[rows, im_l] = tr * hi_ - ti * hr
            at = slice(chans * block + q * half, chans * block + (q + 1) * half)
            work[at, re_l] = jnp.where(line_of == c, folded(gr * hr + gi * hi_), work[at, re_l])
            work[at, im_l] = jnp.where(line_of == c, folded(gr * hi_ - gi * hr), work[at, im_l])

    multiply(work, chans * block, block, tables_ref, 2)
    for m, (re, im) in enumerate(load_inverse(work, chans * block)):
        outgoing[m] = re

    def sum_copy(o, slot, target):
        return pltpu.make_async_remote_copy(
            src_ref=outgoing.at[target % outer], dst_ref=incoming.at[slot],
            send_sem=sum_send.at[o], recv_sem=sum_recv.at[slot],
            device_id=place(target), device_id_type=MESH)

    @pl.loop(1, n)
    def _(o):
        sum_copy(o, me, (me + o) % n).start()

    incoming[me] = outgoing[me % outer]
    partial[...] = jnp.zeros(partial.shape, jnp.float32)

    @pl.loop(0, chans)
    def _(c):
        sums = [jnp.zeros((half, LANES), jnp.float32) for _ in range(10)]
        for m in range(outer):
            for rows in (lo, hi):
                grad = back[c, rows, cols(m)] * slope[c, rows, cols(m)]
                for t in range(9):
                    sums[t] = sums[t] + grad * proj_shift[t, rows, cols(m)]
                sums[9] = sums[9] + grad
        for t in range(10):
            partial[c, t : t + 1, :] = folded(sums[t])

    for s in range(0, chans * block, step):
        multiply(work, s, step, tables_ref, 2)

    @pl.loop(0, chans)
    def _(c):
        sums = [jnp.zeros((half, LANES), jnp.float32) for _ in range(9)]
        for m, (re, im) in enumerate(load_inverse(work, start_of(c))):
            filt[c, lo, cols(m)] = re
            filt[c, hi, cols(m)] = im
            for t in range(9):
                sums[t] = sums[t] + re * cot_shift[t, lo, cols(m)] + im * cot_shift[t, hi, cols(m)]
        for t in range(9):
            partial[c, 16 + t : 17 + t, :] = folded(sums[t])

    small = lax.dot_general(
        jnp.ones((8, LANES), jnp.float32), partial[...].reshape(chans * SLOTS, LANES),
        (((1,), (1,)), ((), ())),
        precision=lax.Precision.HIGHEST, preferred_element_type=jnp.float32)
    width = chans_dev * SLOTS
    for h in range(ch_n):
        small_own[h] = small[0:1, h * width : (h + 1) * width]

    def small_copy(o, slot, target):
        return pltpu.make_async_remote_copy(
            src_ref=small_own.at[target % ch_n], dst_ref=small_in.at[slot],
            send_sem=small_send.at[o], recv_sem=small_recv.at[slot],
            device_id=place(target), device_id_type=MESH)

    @pl.loop(1, n)
    def _(o):
        small_copy(o, me, (me + o) % n).start()

    small_in[me] = small_own[c0]

    @pl.loop(1, n)
    def _(o):
        source = (me + o) % n
        sum_copy(o, source, source).wait_recv()

    total = incoming[0]
    for d in range(1, n):
        total = total + incoming[d]
    mine = me % outer
    group = me - mine
    collected[mine] = total

    def gather_copy(o, slot, target):
        return pltpu.make_async_remote_copy(
            src_ref=collected.at[mine], dst_ref=collected.at[slot],
            send_sem=gather_send.at[o], recv_sem=gather_recv.at[slot],
            device_id=place(group + target), device_id_type=MESH)

    @pl.loop(1, outer)
    def _(o):
        gather_copy(o, mine, (mine + o) % outer).start()

    @pl.loop(0, outer)
    def _(m):
        at = pl.ds(pl.multiple_of(m * LANES, LANES), LANES)
        for rows in (lo, hi):
            pieces = [filt[c, rows, at] for c in range(chans)]
            for t in range(9):
                total = second_ref[t // 3, t % 3, 0] * pieces[0]
                for c in range(1, chans):
                    total = total + second_ref[t // 3, t % 3, c] * pieces[c]
                mixed[t, rows, at] = total

    sides = []
    for j in range(3):
        total = mixed[3 + j]
        for i in (0, 2):
            total = total + pltpu.roll(mixed[3 * i + j], -(i - 1) * rq % both, 0)
        sides.append(total)
    image = sides[1] + from_left(sides[0]) + from_right(sides[2])
    for a in range(angles):
        sino_ref[a] = image[a * rq : (a + 1) * rq]

    @pl.loop(1, n)
    def _(o):
        source = (me + o) % n
        small_copy(o, source, source).wait_recv()

    sums = small_in[0]
    for d in range(1, n):
        sums = sums + small_in[d]
    for l in range(chans_dev):
        for i in range(3):
            at = l * SLOTS + 3 * i
            first_out_ref[i, l : l + 1, :] = sums[:, at : at + 3]
            second_out_ref[i, l : l + 1, :] = sums[:, at + 16 : at + 19]
        bias_out_ref[0:1, l : l + 1] = sums[:, l * SLOTS + 9 : l * SLOTS + 10]

    @pl.loop(1, outer)
    def _(o):
        source = (mine + o) % outer
        gather_copy(o, source, source).wait_recv()

    for m in range(outer):
        taps_out_ref[:, cols(m)] = collected[m, pl.ds(c0 * chans_dev, chans_dev), :]

    for o in range(1, ang_n):
        rows_copy(o, z, (z + o) % ang_n).wait_send()
    for o in range(1, ch_n):
        taps_copy(o, c0, (c0 + o) % ch_n).wait_send()
        packed_copy(o, c0, (c0 + o) % ch_n).wait_send()

    @pl.when(sends_top)
    def _():
        top_copy(z).wait_send()

    @pl.when(sends_bottom)
    def _():
        bottom_copy(z).wait_send()

    @pl.loop(1, n)
    def _(o):
        sum_copy(o, me, (me + o) % n).wait_send()
        small_copy(o, me, (me + o) % n).wait_send()

    @pl.loop(1, outer)
    def _(o):
        gather_copy(o, mine, (mine + o) % outer).wait_send()


def deliver(*refs):
    count = (len(refs) - 1) // 3
    sources, targets, staged = refs[:count], refs[count : 2 * count], refs[2 * count : 3 * count]
    sems = refs[-1]
    into = [pltpu.make_async_copy(sources[at], staged[at], sems.at[0, at]) for at in range(count)]
    out = [pltpu.make_async_copy(staged[at], targets[at], sems.at[1, at]) for at in range(count)]
    for copy in into:
        copy.start()
    for copy_in, copy_out in zip(into, out):
        copy_in.wait()
        copy_out.start()
    for copy in out:
        copy.wait()


def on_device(sizes, tables, projections, conv1_weight, conv1_bias, filter_taps, conv2_weight, cotangent):
    ang_n, row_n, ch_n = sizes
    n = ang_n * row_n * ch_n
    _, held, columns = projections.shape
    chans_dev = conv1_weight.shape[0]
    chans = chans_dev * ch_n
    _, angles, rq, _ = cotangent.shape
    outer = columns // LANES
    both = angles * rq
    block = outer * both // 2
    f32 = jnp.float32
    vmem = pl.BlockSpec(memory_space=pltpu.VMEM)
    hbm = pl.BlockSpec(memory_space=pltpu.HBM)
    dma = pltpu.SemaphoreType.DMA
    wide = (both, columns)
    shapes = (
        jax.ShapeDtypeStruct((angles, rq, columns), f32),
        jax.ShapeDtypeStruct((3, chans_dev, 3), f32),
        jax.ShapeDtypeStruct((1, chans_dev), f32),
        jax.ShapeDtypeStruct((chans_dev, columns), f32),
        jax.ShapeDtypeStruct((3, chans_dev, 3), f32),
    )
    results = pl.pallas_call(
        functools.partial(kernel, sizes),
        out_shape=shapes,
        in_specs=[hbm] * 4 + [pl.BlockSpec(memory_space=pltpu.SMEM)] + [hbm] * 3,
        out_specs=(vmem,) * 5,
        scratch_shapes=[
            pltpu.VMEM((held, columns), f32),
            pltpu.VMEM((3, chans_dev, 3), f32),
            pltpu.VMEM((1, chans_dev), f32),
            pltpu.VMEM((chans_dev, columns), f32),
            pltpu.VMEM((angles, rq, columns), f32),
            pltpu.VMEM(tables[0].shape, jnp.bfloat16),
            pltpu.VMEM(tables[1].shape, f32),
            pltpu.VMEM(((held + 2) * outer, LANES), f32),
            pltpu.VMEM((chans_dev, LANES), f32),
            pltpu.VMEM((n, 1, LANES), f32),
            pltpu.VMEM((ch_n, 1, LANES), f32),
            pltpu.VMEM((ang_n, (rq + 2) * outer, LANES), f32),
            pltpu.VMEM((ang_n, outer, LANES), f32),
            pltpu.VMEM((ang_n, outer, LANES), f32),
            pltpu.VMEM((ch_n, chans_dev, columns), f32),
            pltpu.VMEM((ch_n, chans_dev, LANES), f32),
            pltpu.SMEM((ch_n, chans_dev, LANES), f32),
            pltpu.VMEM((9,) + wide, f32),
            pltpu.VMEM((9,) + wide, f32),
            pltpu.VMEM((chans * block, 2 * LANES), f32),
            pltpu.VMEM((chans * block, 2 * LANES), f32),
            pltpu.VMEM((block, 2 * LANES), f32),
            pltpu.VMEM(((chans + 1) * block, 2 * LANES), f32),
            pltpu.VMEM((chans,) + wide, f32),
            pltpu.VMEM((chans,) + wide, f32),
            pltpu.VMEM((chans,) + wide, f32),
            pltpu.VMEM((chans, SLOTS, LANES), f32),
            pltpu.VMEM((9,) + wide, f32),
            pltpu.VMEM((outer, chans, LANES), f32),
            pltpu.VMEM((n, chans, LANES), f32),
            pltpu.VMEM((outer, chans, LANES), f32),
            dma((ang_n,)), dma((ang_n,)), dma((2,)), dma((2, ang_n)),
            dma((ch_n,)), dma((ch_n,)), dma((ch_n,)), dma((ch_n,)),
            dma((n,)), dma((n,)), dma((outer,)), dma((outer,)),
            dma((n,)), dma((n,)), dma((7,)), dma(()),
        ],
        compiler_params=pltpu.CompilerParams(
            collective_id=0, has_side_effects=True, vmem_limit_bytes=63 * 2**20
        ),
        name="tomography",
    )(
        projections[0], jnp.transpose(conv1_weight, (1, 0, 2)), conv1_bias[None], filter_taps,
        jnp.transpose(conv2_weight, (1, 2, 0)), cotangent[0], *tables,
    )
    image, first, bias, taps_out, second = pl.pallas_call(
        deliver,
        out_shape=shapes,
        in_specs=[hbm] * 5,
        out_specs=(hbm,) * 5,
        scratch_shapes=[pltpu.VMEM(leaf.shape, f32) for leaf in shapes] + [dma((2, 5))],
        compiler_params=pltpu.CompilerParams(vmem_limit_bytes=63 * 2**20),
        name="deliver",
    )(*results)
    return (
        image[None], jnp.transpose(first, (1, 0, 2)), bias[0], taps_out,
        jnp.transpose(second, (1, 0, 2)),
    )


def solution(mesh):
    sizes = tuple(mesh.shape[axis] for axis in ("ang", "row", "ch"))

    def whole(projections, conv1_weight, conv1_bias, filter_taps, conv2_weight, cotangent):
        tables = make_tables(projections.shape[-1])

        def local(*arrays):
            return on_device(sizes, tuple(jnp.asarray(t) for t in tables), *arrays)

        return jax.shard_map(
            local,
            mesh=mesh,
            in_specs=(
                P(("slab", "ang"), "row", None),
                P("ch", None, None),
                P("ch"),
                P("ch", None),
                P(),
                P(("slab", "row"), None, ("ang", "ch"), None),
            ),
            out_specs=(
                P(("slab", "row"), None, ("ang", "ch"), None),
                P(("slab", "ch"), None, None),
                P(("slab", "ch")),
                P(("slab", "ch"), None),
                P(("slab", "ch"), None, None),
            ),
            check_vma=False,
        )(projections, conv1_weight, conv1_bias, filter_taps, conv2_weight, cotangent)

    return whole
```
